32 devices in a mesh: dp: 4 (over x, core), seq: 8 (over z, y).
Axes of the slice: x: 2, y: 2, z: 4, core: 2. Of those that a mesh axis runs over, the one named last changes fastest.
Arguments:
- queries: bfloat16 [8192, 16, 128], P(('dp', 'seq')), parts along dimension 0, may hold values from -6 to 6
- keys: bfloat16 [8192, 16, 128], P(('dp', 'seq')), parts along dimension 0, may hold values from -6 to 6
- values: bfloat16 [8192, 16, 128], P(('dp', 'seq')), parts along dimension 0, may hold values from -6 to 6
- cotangent: bfloat16 [8192, 16, 128], P(('dp', 'seq')), parts along dimension 0, may hold values from -6 to 6
- doc_lengths: int32 [96], P('dp'), parts along dimension 0, may hold values from 1 to 512, 2048 in all
Outputs:
- attended: bfloat16 [8192, 16, 128], P(('dp', 'seq')), parts along dimension 0
- grad_queries: bfloat16 [8192, 16, 128], P(('dp', 'seq')), parts along dimension 0
- grad_keys: bfloat16 [8192, 16, 128], P(('dp', 'seq')), parts along dimension 0
- grad_values: bfloat16 [8192, 16, 128], P(('dp', 'seq')), parts along dimension 0
The draws below stay inside these ranges and needn't reach their ends.
There are 4 independent parts, one for each index of `dp`. The reference program is written for one: setup_inputs(seed, part) draws one part's arguments, and reference() takes and returns one part's arrays. A program takes and returns all parts, laid end to end along the dimension named above; each array names one. Nothing has to cross between parts.
Inputs may be any that keep to these rules, and one draw needn't show every extreme that they name: `doc_lengths`: the lengths sum to 2048, and the longest document has exactly 512 positions.
All inputs are finite; a program needn't handle non-finite values.
Results may differ from the reference program's by a relative error of at most 0.005.
Values sent between devices are 32-bit elements; how exact they have to be, the bound alone decides.
A program may use at most 64 MiB of HBM per device.

```python
import math
import jax
import jax.numpy as jnp
import numpy as np
from jax import lax

HEADS = 16
DK = 128
DV = 128
BLOCK = 256
DOCS = 24
TOKENS = 2048
MOST = 512


def shard_levels(own_key, extent, cuts, least, largest):
    level = 1.0
    for axis_at, blocks in cuts:
        draws = jax.random.uniform(jax.random.fold_in(jax.random.fold_in(own_key, 6), axis_at), (blocks,), jnp.float32, least / len(cuts), largest / len(cuts))
        level = level * jnp.repeat(jnp.exp(draws), extent[axis_at] // blocks).reshape((-1,) + (1,) * (len(extent) - 1 - axis_at))
    return level


def profile(count, total, most, skew):
    weights = [(1 << 20) // math.isqrt(grade ** skew) + 1 for grade in range(2, count + 1)]
    spare, given = total - most - (count - 1), [1] * (count - 1)
    while spare > 0:
        candidates = [i for i in range(count - 1) if given[i] < most]
        whole, remaining = sum([weights[i] for i in candidates]), spare
        for i in candidates:
            more = min(most - given[i], max(1, remaining * weights[i] // whole), spare)
            given[i] = given[i] + more
            spare = spare - more
    return np.array([most] + given)


def uneven(stream_key, amount, total, bound, skew):
    if amount == 2:
        one = jax.random.randint(stream_key, (), max(1, total - bound), min(bound, total - 1) + 1)
        return jnp.stack([one, total - one])
    lengths = jnp.asarray(profile(amount, total, bound, skew), jnp.int32)
    pairs = (amount - 1) // 2
    donor, sink = lengths[1:1 + 2 * pairs:2], lengths[2:2 + 2 * pairs:2]
    margin = jnp.minimum(donor - 1, bound - sink)
    moved = jax.random.randint(jax.random.fold_in(stream_key, 1), (pairs,), 0, 1 << 20) % (margin + 1)
    lengths = lengths.at[1:1 + 2 * pairs:2].set(donor - moved).at[2:2 + 2 * pairs:2].set(sink + moved)
    return lengths[jax.random.permutation(jax.random.fold_in(stream_key, 2), amount)]


def bell_draw(rng, shape, scale, reach, shards=(), kind=jnp.bfloat16):
    array = scale * jax.random.normal(rng, shape, jnp.float32)
    if shards:
        array = array * shard_levels(rng, shape, shards, -0.22, 0.18)
    return jnp.clip(array, -reach, reach).astype(kind)


def setup_inputs(seed: int = 0, part: int = 0) -> dict:
    key_of = jax.random.split(jax.random.key(seed), 6)
    part_splits = jax.random.split(jax.random.fold_in(key_of[5], part), 6)
    return {
        "queries": bell_draw(part_splits[0], (TOKENS, HEADS, DK), 1.0, 6.0, ((0, 8),)),
        "keys": bell_draw(part_splits[1], (TOKENS, HEADS, DK), 1.0, 6.0, ((0, 8),)),
        "values": bell_draw(part_splits[2], (TOKENS, HEADS, DV), 1.0, 6.0, ((0, 8),)),
        "cotangent": bell_draw(part_splits[3], (TOKENS, HEADS, DV), 1.0, 6.0, ((0, 8),)),
        "doc_lengths": uneven(part_splits[4], DOCS, TOKENS, MOST, 2).astype(jnp.int32),
    }


def doc_index(doc_lengths):
    doc_ends = jnp.cumsum(doc_lengths).astype(jnp.int32)
    positions = jnp.arange(TOKENS, dtype=jnp.int32)
    return jnp.sum((positions[:, None] >= doc_ends[None, :]).astype(jnp.int32), axis=1).astype(jnp.int32)


def block_outputs(pieces):
    query_blk, key_blk, value_blk, cot_blk, block_ids, state_in, return_in = pieces
    factor = (DK * BLOCK) ** -0.5
    places = jnp.arange(BLOCK, dtype=jnp.int32)
    visible = (block_ids[:, None] == block_ids[None, :]) & (places[:, None] >= places[None, :])
    query_f = query_blk.astype(jnp.float32)
    key_f = key_blk.astype(jnp.float32)
    value_f = value_blk.astype(jnp.float32)
    cot_f = cot_blk.astype(jnp.float32)
    scores = jnp.einsum("thd,shd->hts", query_f, key_f)
    weights = jnp.where(visible[None], factor * scores, 0.0).astype(jnp.bfloat16).astype(jnp.float32)
    grad_scores = jnp.einsum("the,she->hts", cot_f, value_f)
    grad_weights = jnp.where(visible[None], factor * grad_scores, 0.0).astype(jnp.bfloat16).astype(jnp.float32)
    head_in = (block_ids == block_ids[0]).astype(jnp.float32)[:, None, None]
    tail_in = (block_ids == block_ids[-1]).astype(jnp.float32)[:, None, None]
    state_f = state_in.astype(jnp.float32)
    return_f = return_in.astype(jnp.float32)
    attended = jnp.einsum("hts,she->the", weights, value_f) + factor * head_in * jnp.einsum("thd,hde->the", query_f, state_f)
    grad_q = jnp.einsum("hts,shd->thd", grad_weights, key_f) + factor * head_in * jnp.einsum("the,hde->thd", cot_f, state_f)
    grad_k = jnp.einsum("hts,thd->shd", grad_weights, query_f) + factor * tail_in * jnp.einsum("she,hde->shd", value_f, return_f)
    grad_v = jnp.einsum("hts,the->she", weights, cot_f) + factor * tail_in * jnp.einsum("shd,hde->she", key_f, return_f)
    return (attended.astype(jnp.bfloat16), grad_q.astype(jnp.bfloat16), grad_k.astype(jnp.bfloat16), grad_v.astype(jnp.bfloat16))


def reference(queries, keys, values, cotangent, doc_lengths):
    ident = doc_index(doc_lengths)
    count = TOKENS // BLOCK
    query_b = queries.reshape(count, BLOCK, HEADS, DK)
    key_b = keys.reshape(count, BLOCK, HEADS, DK)
    value_b = values.reshape(count, BLOCK, HEADS, DV)
    cot_b = cotangent.reshape(count, BLOCK, HEADS, DV)
    id_b = ident.reshape(count, BLOCK)
    next_first = jnp.concatenate([id_b[1:, 0], jnp.full((1,), -1, jnp.int32)])
    prev_last = jnp.concatenate([jnp.full((1,), -1, jnp.int32), id_b[:-1, -1]])
    zero_state = jnp.zeros((HEADS, DK, DV), jnp.float32)

    def forward_step(running, pieces):
        key_blk, value_blk, block_ids, target = pieces
        masked = jnp.where((block_ids == target)[:, None, None], key_blk.astype(jnp.float32), 0.0)
        addend = jnp.einsum("shd,she->hde", masked, value_blk.astype(jnp.float32))
        keep_on = (block_ids[0] == target).astype(jnp.float32)
        return addend + keep_on * running, running

    def backward_step(running, pieces):
        query_blk, cot_blk, block_ids, target = pieces
        masked = jnp.where((block_ids == target)[:, None, None], query_blk.astype(jnp.float32), 0.0)
        addend = jnp.einsum("thd,the->hde", masked, cot_blk.astype(jnp.float32))
        keep_on = (block_ids[-1] == target).astype(jnp.float32)
        return addend + keep_on * running, running

    _, state_sum = lax.scan(forward_step, zero_state, (key_b, value_b, id_b, next_first))
    _, return_sum = lax.scan(backward_step, zero_state, (query_b, cot_b, id_b, prev_last), reverse=True)
    carried = state_sum.astype(jnp.bfloat16)
    returned = return_sum.astype(jnp.bfloat16)
    attended, grad_q, grad_k, grad_v = lax.map(block_outputs, (query_b, key_b, value_b, cot_b, id_b, carried, returned))
    return (attended.reshape(TOKENS, HEADS, DV), grad_q.reshape(TOKENS, HEADS, DK), grad_k.reshape(TOKENS, HEADS, DK), grad_v.reshape(TOKENS, HEADS, DV))
```

```python
import functools

import jax
import jax.numpy as jnp
from jax import lax
from jax.experimental import pallas as pl
from jax.experimental.pallas import tpu as pltpu
from jax.sharding import PartitionSpec as P

BLOCK = 256
LONGEST_PART = 4
MESH = pl.DeviceIdType.MESH
INNER_LAG, OUTER_LAG = 3, 5
LOAD_PARTS, STORE_PARTS = 4, 4


def dot(a, b, ca, cb):
    return lax.dot_general(
        a, b, (((ca,), (cb,)), ((), ())), preferred_element_type=jnp.float32
    )


def kernel(
    seq, hops,
    lengths, q_hbm, k_hbm, v_hbm, c_hbm,
    att_out, gq_out, gk_out, gv_out,
    q_in, k_in, v_in, c_in, qf, kf, vf, cf, qh, kh, vh, ch,
    mask, state, ret, state_in, ret_in, relay_in,
    load_sem, relay_send, relay_recv, state_send, state_recv, ret_send, ret_recv,
):
    rows, heads, width = q_in.shape
    loads = [
        pltpu.make_async_copy(src, dst, load_sem.at[i])
        for i, (src, dst) in enumerate(
            ((k_hbm, k_in), (v_hbm, v_in), (q_hbm, q_in), (c_hbm, c_in))
        )
    ]
    for load in loads:
        load.start()
    factor = (width * BLOCK) ** (-0.5)
    dp, me = lax.axis_index("dp"), lax.axis_index("seq")
    first = me * rows
    last = first + rows - 1

    barrier = pltpu.get_barrier_semaphore()
    for d in range(1, hops + 1):
        for ok, peer in ((me + d < seq, me + d), (me - d >= 0, me - d)):
            @pl.when(ok)
            def _(peer=peer):
                pl.semaphore_signal(barrier, inc=1, device_id=(dp, peer), device_id_type=MESH)

    for d in range(hops):
        @pl.when(me - d - 1 < 0)
        def _(d=d):
            state_in[d] = jnp.zeros(state_in.shape[1:], state_in.dtype)

        @pl.when(me + d + 1 >= seq)
        def _(d=d):
            ret_in[d] = jnp.zeros(ret_in.shape[1:], ret_in.dtype)

    big = jnp.int32(2**30)
    zero = jnp.int32(0)
    ends = []
    total = zero
    for j in range(lengths.shape[0]):
        total = total + lengths[j]
        ends.append(total)

    def start_of(p):
        out = zero
        for e in ends:
            out = jnp.maximum(out, jnp.where(e <= p, e, zero))
        return out

    def end_of(p):
        out = big
        for e in ends:
            out = jnp.minimum(out, jnp.where(e > p, e, big))
        return out

    tail_start = start_of(last + 1)
    head_end_prev = end_of(first - 1)
    head_start, head_end = start_of(first), end_of(first)
    last_start, last_end = start_of(last), end_of(last)

    step = 16

    def widen(*pairs):
        def part(i, _):
            at = pl.multiple_of(i * step, step)
            for src, dst in pairs:
                block = src[pl.ds(at, step)].astype(jnp.float32)
                dst[pl.ds(at * heads, step * heads), :] = block.reshape(step * heads, width)
            return 0

        lax.fori_loop(0, rows // step, part, 0)

    pl.semaphore_wait(barrier, jnp.minimum(me, hops) + jnp.minimum(seq - 1 - me, hops))

    pos = first + lax.broadcasted_iota(jnp.int32, (rows, width), 0)
    in_tail = pos >= tail_start
    in_head = pos < head_end_prev

    def forward(d, h):
        return pltpu.make_async_remote_copy(
            src_ref=state.at[h], dst_ref=state_in.at[d, h],
            send_sem=state_send.at[d, h], recv_sem=state_recv.at[d, h],
            device_id=(dp, me + d + 1), device_id_type=MESH,
        )

    def backward(d, h):
        return pltpu.make_async_remote_copy(
            src_ref=ret.at[h], dst_ref=ret_in.at[d, h],
            send_sem=ret_send.at[d, h], recv_sem=ret_recv.at[d, h],
            device_id=(dp, me - d - 1), device_id_type=MESH,
        )

    levels = max(seq // 2, 1)
    odd = lax.rem(me, 2) == 1
    even = lax.rem(me, 2) == 0
    level = me // 2
    up, down = me + 1 < seq, me >= 1

    def state_turn(h):
        return lax.rem(h, levels) < levels - 1 - level

    def ret_turn(h):
        return lax.rem(h, levels) < level

    def state_via(h):
        return odd & up & state_turn(h)

    def state_relays(h):
        return even & (me + 2 < seq) & state_turn(h)

    def ret_via(h):
        return even & (me >= 2) & up & ret_turn(h)

    def ret_relays(h):
        return odd & (me >= 2) & ret_turn(h)

    def via_state(h):
        return pltpu.make_async_remote_copy(
            src_ref=state.at[h], dst_ref=relay_in.at[0, h],
            send_sem=state_send.at[0, h], recv_sem=relay_recv.at[0, h],
            device_id=(dp, me - 1), device_id_type=MESH,
        )

    def via_ret(h):
        return pltpu.make_async_remote_copy(
            src_ref=ret.at[h], dst_ref=relay_in.at[1, h],
            send_sem=ret_send.at[0, h], recv_sem=relay_recv.at[1, h],
            device_id=(dp, me + 1), device_id_type=MESH,
        )

    def relay_state(h):
        return pltpu.make_async_remote_copy(
            src_ref=relay_in.at[0, h], dst_ref=state_in.at[0, h],
            send_sem=relay_send.at[0, h], recv_sem=state_recv.at[0, h],
            device_id=(dp, me + 2), device_id_type=MESH,
        )

    def relay_ret(h):
        return pltpu.make_async_remote_copy(
            src_ref=relay_in.at[1, h], dst_ref=ret_in.at[0, h],
            send_sem=relay_send.at[1, h], recv_sem=ret_recv.at[0, h],
            device_id=(dp, me - 2), device_id_type=MESH,
        )

    def sends_state(d, h):
        if d == 0 and hops > 1:
            return up & jnp.logical_not(state_via(h))
        return me + d + 1 < seq

    def sends_ret(d, h):
        if d == 0 and hops > 1:
            return down & jnp.logical_not(ret_via(h))
        return me - d - 1 >= 0

    def arrived_state(h):
        return pltpu.make_async_remote_copy(
            src_ref=state.at[h], dst_ref=relay_in.at[0, h],
            send_sem=state_send.at[0, h], recv_sem=relay_recv.at[0, h],
            device_id=(dp, me + 1), device_id_type=MESH,
        )

    def arrived_ret(h):
        return pltpu.make_async_remote_copy(
            src_ref=ret.at[h], dst_ref=relay_in.at[1, h],
            send_sem=ret_send.at[0, h], recv_sem=relay_recv.at[1, h],
            device_id=(dp, me - 1), device_id_type=MESH,
        )

    def relay(h):
        if hops > 1:
            @pl.when(state_relays(h))
            def _():
                arrived_state(h).wait_recv()
                relay_state(h).start()

            @pl.when(ret_relays(h))
            def _():
                arrived_ret(h).wait_recv()
                relay_ret(h).start()

    def state_sum(h):
        k32 = kf[pl.ds(h, rows, stride=heads), :]
        v16 = vf[pl.ds(h, rows, stride=heads), :].astype(jnp.bfloat16)
        kh[h] = k32.astype(jnp.bfloat16)
        vh[h] = v16
        state[h] = dot(jnp.where(in_tail, k32, 0.0).astype(jnp.bfloat16), v16, 0, 0)
        if hops > 1:
            @pl.when(state_via(h))
            def _():
                via_state(h).start()

        for d in range(hops):
            @pl.when(sends_state(d, h))
            def _(d=d):
                forward(d, h).start()

    def ret_sum(h):
        q32 = qf[pl.ds(h, rows, stride=heads), :]
        c16 = cf[pl.ds(h, rows, stride=heads), :].astype(jnp.bfloat16)
        qh[h] = q32.astype(jnp.bfloat16)
        ch[h] = c16
        ret[h] = dot(jnp.where(in_head, q32, 0.0).astype(jnp.bfloat16), c16, 0, 0)
        if hops > 1:
            @pl.when(ret_via(h))
            def _():
                via_ret(h).start()

        for d in range(hops):
            @pl.when(sends_ret(d, h))
            def _(d=d):
                backward(d, h).start()

    def each(fn):
        def body(h, _):
            fn(h)
            return 0

        return body

    ahead = min(4, heads)
    loads[0].wait()
    loads[1].wait()
    widen((k_in, kf), (v_in, vf))
    lax.fori_loop(0, ahead, each(state_sum), 0)
    loads[2].wait()
    loads[3].wait()
    widen((q_in, qf), (c_in, cf))

    def both(h):
        ret_sum(h)
        state_sum(h + ahead)

    lax.fori_loop(0, heads - ahead, each(both), 0)
    lax.fori_loop(heads - ahead, heads, each(ret_sum), 0)

    t_pos = first + lax.broadcasted_iota(jnp.int32, (rows, rows), 0)
    s_pos = first + lax.broadcasted_iota(jnp.int32, (rows, rows), 1)
    col = first + lax.broadcasted_iota(jnp.int32, (rows, 1), 0)
    begin = jnp.zeros((rows, 1), jnp.int32)
    for e in ends:
        begin = jnp.maximum(begin, jnp.where(col >= e, e, 0))
    visible = (s_pos <= t_pos) & (s_pos >= begin)
    mask[...] = jnp.where(visible, factor, 0.0).astype(jnp.float32)

    lead = heads // 8

    def inside(h, _):
        @pl.when(h >= heads // 2 - lead)
        def _():
            relay(h - (heads // 2 - lead))

        q, k, v, c = qh[h], kh[h], vh[h], ch[h]
        m = mask[...]
        weights = (m * dot(q, k, 1, 1)).astype(jnp.bfloat16)
        grad_weights = (m * dot(c, v, 1, 1)).astype(jnp.bfloat16)
        spot = pl.ds(h, rows, stride=heads)
        qf[spot, :] = dot(weights, v, 1, 0)
        kf[spot, :] = dot(grad_weights, k, 1, 0)
        vf[spot, :] = dot(grad_weights, q, 0, 0)
        cf[spot, :] = dot(weights, c, 0, 0)
        return 0

    lax.fori_loop(0, heads, inside, 0)

    head_factor = jnp.where(pos < head_end, factor, 0.0).astype(jnp.float32)
    tail_factor = jnp.where(pos >= last_start, factor, 0.0).astype(jnp.float32)

    def outside(h, _):
        carried = jnp.zeros((width, width), jnp.float32)
        returned = jnp.zeros((width, width), jnp.float32)
        @pl.when((h >= heads - heads // 2) & (h + lead < heads))
        def _():
            relay(h + lead)

        for d in range(hops):
            @pl.when(me - d - 1 >= 0)
            def _(d=d):
                forward(d, h).wait_recv()

            @pl.when(me + d + 1 < seq)
            def _(d=d):
                backward(d, h).wait_recv()

            here = head_start <= first - d * rows
            carried = carried + jnp.where(here, state_in[d, h], 0.0)
            there = last_end >= last + d * rows + 1
            returned = returned + jnp.where(there, ret_in[d, h], 0.0)
        carried = carried.astype(jnp.bfloat16)
        returned = returned.astype(jnp.bfloat16)
        q, k, v, c = qh[h], kh[h], vh[h], ch[h]
        spot = pl.ds(h, rows, stride=heads)
        qf[spot, :] = qf[spot, :] + head_factor * dot(q, carried, 1, 0)
        kf[spot, :] = kf[spot, :] + head_factor * dot(c, carried, 1, 1)
        vf[spot, :] = vf[spot, :] + tail_factor * dot(v, returned, 1, 1)
        cf[spot, :] = cf[spot, :] + tail_factor * dot(k, returned, 1, 0)
        return 0

    lax.fori_loop(0, heads, outside, 0)

    def narrow(i, _):
        at = pl.multiple_of(i * step, step)
        for src, dst in ((qf, att_out), (kf, gq_out), (vf, gk_out), (cf, gv_out)):
            block = src[pl.ds(at * heads, step * heads), :].reshape(step, heads, width)
            dst[pl.ds(at, step)] = block.astype(jnp.bfloat16)
        return 0

    lax.fori_loop(0, rows // step, narrow, 0)

    def drain(h):
        for d in range(hops):
            @pl.when(sends_state(d, h))
            def _(d=d):
                forward(d, h).wait_send()

            @pl.when(sends_ret(d, h))
            def _(d=d):
                backward(d, h).wait_send()

        if hops > 1:
            @pl.when(state_via(h))
            def _():
                via_state(h).wait_send()

            @pl.when(ret_via(h))
            def _():
                via_ret(h).wait_send()

            @pl.when(state_relays(h))
            def _():
                relay_state(h).wait_send()

            @pl.when(ret_relays(h))
            def _():
                relay_ret(h).wait_send()

    lax.fori_loop(0, heads, each(drain), 0)


def paired(
    seq,
    lens_hbm, q_hbm, k_hbm, v_hbm, c_hbm,
    o1, o2, o3, o4,
    lengths, xa_in, xb_in, pa_in, pb_in, xa_h, xb_h, pa_h, pb_h,
    mask, x_rows, p_rows, x_scale, p_scale,
    x_out, p_raw, p_sum, near_in, far_in, pair_in, relay_in,
    len_sem, load_sem, near_send, near_recv, far_send, far_recv,
    pair_send, pair_recv, relay_send, relay_recv,
):
    rows, heads, width = xa_in.shape
    factor = (width * BLOCK) ** (-0.5)
    dp, me = lax.axis_index("dp"), lax.axis_index("seq")
    odd = lax.rem(me, 2) == 1
    even = jnp.logical_not(odd)
    toward = jnp.where(odd, 1, -1)
    first = me * rows
    last = first + rows - 1
    parts = load_sem.shape[1]
    span = rows // parts

    len_load = pltpu.make_async_copy(lens_hbm, lengths, len_sem)
    len_load.start()

    def load(i, part, src, dst):
        cut = pl.ds(part * span, span)
        return pltpu.make_async_copy(src.at[cut], dst.at[cut], load_sem.at[i, part])

    landing = (xa_in, xb_in, pa_in, pb_in)

    @pl.when(even)
    def _():
        for pair in (0, 2):
            for part in range(parts):
                for i in (pair, pair + 1):
                    load(i, part, (q_hbm, c_hbm, k_hbm, v_hbm)[i], landing[i]).start()

    @pl.when(odd)
    def _():
        for pair in (0, 2):
            for part in range(parts):
                for i in (pair, pair + 1):
                    load(i, part, (k_hbm, v_hbm, q_hbm, c_hbm)[i], landing[i]).start()

    near, pair = me + toward, me - toward
    far_to, far_from = me - 2 * toward, me + 2 * toward
    near_ok = (near >= 0) & (near < seq)
    far_to_ok = (far_to >= 0) & (far_to < seq)
    far_from_ok = (far_from >= 0) & (far_from < seq)

    barrier = pltpu.get_barrier_semaphore()
    for ok, peer in ((near_ok, near), (pair >= 0, pair), (far_to_ok, far_to), (far_from_ok, far_from)):
        @pl.when(ok)
        def _(peer=peer):
            pl.semaphore_signal(barrier, inc=1, device_id=(dp, peer), device_id_type=MESH)

    @pl.when(jnp.logical_not(near_ok))
    def _():
        near_in[...] = jnp.zeros(near_in.shape, near_in.dtype)

    @pl.when(jnp.logical_not(far_from_ok))
    def _():
        far_in[...] = jnp.zeros(far_in.shape, far_in.dtype)

    len_load.wait()
    big = jnp.int32(2**30)
    zero = jnp.int32(0)
    ends = []
    total = zero
    for j in range(lengths.shape[0]):
        total = total + lengths[j]
        ends.append(total)

    def start_of(p):
        out = zero
        for e in ends:
            out = jnp.maximum(out, jnp.where(e <= p, e, zero))
        return out

    def end_of(p):
        out = big
        for e in ends:
            out = jnp.minimum(out, jnp.where(e > p, e, big))
        return out

    tail_start = start_of(last + 1)
    head_end_prev = end_of(first - 1)
    head_start, head_end = start_of(first), end_of(first)
    last_start, last_end = start_of(last), end_of(last)
    x_keep = jnp.where(odd, last_end >= last + rows + 1, head_start <= first - rows)
    p_keep = jnp.where(odd, head_end_prev >= last + 1, tail_start <= first)

    pos = first + lax.broadcasted_iota(jnp.int32, (rows, width), 0)
    x_low, x_high = jnp.where(odd, tail_start, zero), jnp.where(odd, big, head_end_prev)
    p_low, p_high = jnp.where(odd, zero, tail_start), jnp.where(odd, head_end_prev, big)
    x_rows[...] = jnp.where((pos >= x_low) & (pos < x_high), 1.0, 0.0).astype(jnp.bfloat16)

    step = 16

    def widen(part, *pairs):
        def some(i, _):
            at = pl.multiple_of(part * span + i * step, step)
            for src, dst in pairs:
                block = src[pl.ds(at, step)].astype(jnp.float32)
                dst[pl.ds(at * heads, step * heads), :] = block.reshape(step * heads, width)
            return 0

        lax.fori_loop(0, span // step, some, 0)

    levels = seq // 2
    level = me // 2
    mine = jnp.where(odd, levels - 1 - level, level)
    theirs = levels - 1 - mine

    def my_turn(h):
        return lax.rem(h, levels) < mine

    def their_turn(h):
        return lax.rem(h, levels) < theirs

    def remote(src, dst, send, recv, peer):
        return pltpu.make_async_remote_copy(
            src_ref=src, dst_ref=dst, send_sem=send, recv_sem=recv,
            device_id=(dp, peer), device_id_type=MESH,
        )

    def direct(h):
        return remote(x_out.at[h], near_in.at[h], near_send.at[h], near_recv.at[h], near)

    def via(h):
        return remote(x_out.at[h], relay_in.at[h], near_send.at[h], relay_recv.at[h], pair)

    def onward(h):
        return remote(relay_in.at[h], near_in.at[h], relay_send.at[h], near_recv.at[h], far_to)

    def far(h):
        return remote(p_raw.at[h], far_in.at[h], far_send.at[h], far_recv.at[h], far_to)

    def across(h):
        return remote(p_sum.at[h], pair_in.at[h], pair_send.at[h], pair_recv.at[h], pair)

    for part in range(parts):
        for i in (0, 1):
            load(i, part, q_hbm, landing[i]).wait()
        widen(part, (xa_in, o1), (xb_in, o2))

    pl.semaphore_wait(
        barrier, 1 + near_ok.astype(jnp.int32) + far_to_ok.astype(jnp.int32) + far_from_ok.astype(jnp.int32)
    )

    def x_state(h, _):
        spot = pl.ds(h, rows, stride=heads)
        xa = o1[spot, :].astype(jnp.bfloat16)
        xb = o2[spot, :].astype(jnp.bfloat16)
        xa_h[h] = xa
        xb_h[h] = xb
        x_out[h] = dot(xa * x_rows[...], xb, 0, 0)

        @pl.when(my_turn(h))
        def _():
            via(h).start()

        @pl.when(near_ok & jnp.logical_not(my_turn(h)))
        def _():
            direct(h).start()

        return 0

    lax.fori_loop(0, heads, x_state, 0)

    p_rows[...] = jnp.where((pos >= p_low) & (pos < p_high), 1.0, 0.0).astype(jnp.bfloat16)
    in_head, in_tail = pos < head_end, pos >= last_start
    head_scale = jnp.where(in_head, factor, 0.0).astype(jnp.float32)
    tail_scale = jnp.where(in_tail, factor, 0.0).astype(jnp.float32)
    x_scale[...] = jnp.where(odd, tail_scale, head_scale)
    p_scale[...] = jnp.where(odd, head_scale, tail_scale)
    col = first + lax.broadcasted_iota(jnp.int32, (1, rows), 1)
    begin = jnp.zeros((1, rows), jnp.int32)
    finish = jnp.full((1, rows), big, jnp.int32)
    for e in ends:
        begin = jnp.maximum(begin, jnp.where(col >= e, e, zero))
        finish = jnp.minimum(finish, jnp.where(col < e, e, big))
    low, high = jnp.where(odd, begin, col), jnp.where(odd, col + 1, finish)
    row = first + lax.broadcasted_iota(jnp.int32, (rows, rows), 0)
    mask[...] = jnp.where((row >= low) & (row < high), factor, 0.0).astype(jnp.float32)

    for part in range(parts):
        for i in (2, 3):
            load(i, part, q_hbm, landing[i]).wait()
        widen(part, (pa_in, o3), (pb_in, o4))

    def p_state(h):
        spot = pl.ds(h, rows, stride=heads)
        pa = o3[spot, :].astype(jnp.bfloat16)
        pb = o4[spot, :].astype(jnp.bfloat16)
        pa_h[h] = pa
        pb_h[h] = pb
        p_raw[h] = dot(pa * p_rows[...], pb, 0, 0)

        @pl.when(far_to_ok)
        def _():
            far(h).start()

    def relay(h):
        @pl.when(their_turn(h))
        def _():
            remote(x_out.at[h], relay_in.at[h], near_send.at[h], relay_recv.at[h], pair).wait_recv()
            onward(h).start()

    def inner(h):
        @pl.when(near_ok)
        def _():
            direct(h).wait_recv()

        p_sum[h] = p_raw[h] + jnp.where(p_keep, near_in[h], 0.0)
        across(h).start()

        @pl.when(far_from_ok)
        def _():
            far(h).wait_recv()

        close = (near_in[h] + jnp.where(x_keep, far_in[h], 0.0)).astype(jnp.bfloat16)
        xa, xb, pa, pb = xa_h[h], xb_h[h], pa_h[h], pb_h[h]
        m = mask[...]
        w1 = (m * dot(xa, pa, 1, 1)).astype(jnp.bfloat16)
        w2 = (m * dot(xb, pb, 1, 1)).astype(jnp.bfloat16)
        spot = pl.ds(h, rows, stride=heads)
        scale = x_scale[...]
        o1[spot, :] = dot(w1, pb, 1, 0) + scale * dot(xa, close, 1, 0)
        o2[spot, :] = dot(w2, pa, 1, 0) + scale * dot(xb, close, 1, 1)
        o3[spot, :] = dot(w2, xa, 0, 0)
        o4[spot, :] = dot(w1, xb, 0, 0)

    def outer(h):
        across(h).wait_recv()
        other = pair_in[h].astype(jnp.bfloat16)
        pa, pb = pa_h[h], pb_h[h]
        spot = pl.ds(h, rows, stride=heads)
        scale = p_scale[...]
        o3[spot, :] = o3[spot, :] + scale * dot(pb, other, 1, 1)
        o4[spot, :] = o4[spot, :] + scale * dot(pa, other, 1, 0)

    inner_lag, outer_lag = INNER_LAG, OUTER_LAG

    def turn(i, _):
        @pl.when(i < heads)
        def _():
            p_state(i)
            relay(i)

        @pl.when((i >= inner_lag) & (i < heads + inner_lag))
        def _():
            inner(i - inner_lag)

        @pl.when(i >= outer_lag)
        def _():
            outer(i - outer_lag)

        return 0

    lax.fori_loop(0, heads + outer_lag, turn, 0)

    def drain(h, _):
        across(h).wait_send()

        @pl.when(near_ok)
        def _():
            direct(h).wait_send()

        @pl.when(far_to_ok)
        def _():
            far(h).wait_send()

        @pl.when(their_turn(h))
        def _():
            onward(h).wait_send()

        return 0

    lax.fori_loop(0, heads, drain, 0)


def settle(i1, i2, i3, i4, att, gq, gk, gv, s1, s2, s3, s4, sem):
    rows, heads, width = s1.shape
    parts = sem.shape[1]
    span = rows // parts
    step = 16
    odd = lax.rem(lax.axis_index("seq"), 2) == 1
    stages = (s1, s2, s3, s4)
    forward, reverse = (att, gq, gk, gv), (gv, gk, gq, att)

    def put(i, part, dst):
        cut = pl.ds(part * span, span)
        return pltpu.make_async_copy(stages[i].at[cut], dst.at[cut], sem.at[i, part])

    for part in range(parts):
        def narrow(i, _):
            at = pl.multiple_of(part * span + i * step, step)
            for src, dst in zip((i1, i2, i3, i4), stages):
                block = src[pl.ds(at * heads, step * heads), :].reshape(step, heads, width)
                dst[pl.ds(at, step)] = block.astype(jnp.bfloat16)
            return 0

        lax.fori_loop(0, span // step, narrow, 0)

        @pl.when(odd)
        def _():
            for i in range(4):
                put(i, part, reverse[i]).start()

        @pl.when(jnp.logical_not(odd))
        def _():
            for i in range(4):
                put(i, part, forward[i]).start()

    for part in range(parts):
        for i in range(4):
            put(i, part, att).wait()


def local_paired(seq, queries, keys, values, cotangent, doc_lengths):
    rows, heads, width = queries.shape
    vmem = pl.BlockSpec(memory_space=pltpu.VMEM)
    hbm = pl.BlockSpec(memory_space=pltpu.HBM)
    whole = pltpu.VMEM((rows, heads, width), jnp.bfloat16)
    by_head = pltpu.VMEM((heads, rows, width), jnp.bfloat16)
    square = pltpu.VMEM((heads, width, width), jnp.float32)
    flat = jax.ShapeDtypeStruct((rows * heads, width), jnp.float32)
    each = pltpu.SemaphoreType.DMA((heads,))
    held = pl.pallas_call(
        functools.partial(paired, seq),
        out_shape=[flat] * 4,
        in_specs=[hbm] * 5,
        out_specs=[vmem] * 4,
        scratch_shapes=[pltpu.SMEM(doc_lengths.shape, jnp.int32)]
        + [whole] * 4
        + [by_head] * 4
        + [pltpu.VMEM((rows, rows), jnp.float32)]
        + [pltpu.VMEM((rows, width), jnp.bfloat16)] * 2
        + [pltpu.VMEM((rows, width), jnp.float32)] * 2
        + [square] * 7
        + [pltpu.SemaphoreType.DMA, pltpu.SemaphoreType.DMA((4, LOAD_PARTS))]
        + [each] * 8,
        compiler_params=pltpu.CompilerParams(
            collective_id=0, has_side_effects=True, vmem_limit_bytes=40 * 2**20
        ),
    )(*(pltpu.with_memory_space_constraint(a, pltpu.HBM) for a in (doc_lengths, queries, keys, values, cotangent)))
    return pl.pallas_call(
        settle,
        out_shape=[jax.ShapeDtypeStruct(queries.shape, jnp.bfloat16)] * 4,
        in_specs=[vmem] * 4,
        out_specs=[hbm] * 4,
        scratch_shapes=[whole] * 4 + [pltpu.SemaphoreType.DMA((4, STORE_PARTS))],
        compiler_params=pltpu.CompilerParams(vmem_limit_bytes=24 * 2**20),
    )(*held)


def local(seq, queries, keys, values, cotangent, doc_lengths):
    rows, heads, width = queries.shape
    longest = seq * rows // LONGEST_PART
    hops = min(seq - 1, (longest - 1 + rows - 1) // rows)
    if hops == 2 and seq % 2 == 0:
        return local_paired(seq, queries, keys, values, cotangent, doc_lengths)
    vmem = pl.BlockSpec(memory_space=pltpu.VMEM)
    flat = pltpu.VMEM((rows * heads, width), jnp.float32)
    by_head = pltpu.VMEM((heads, rows, width), jnp.bfloat16)
    whole = pltpu.VMEM((rows, heads, width), jnp.bfloat16)
    square = pltpu.VMEM((heads, width, width), jnp.float32)
    squares = pltpu.VMEM((hops, heads, width, width), jnp.float32)
    return pl.pallas_call(
        functools.partial(kernel, seq, hops),
        out_shape=[jax.ShapeDtypeStruct(queries.shape, jnp.bfloat16)] * 4,
        in_specs=[pl.BlockSpec(memory_space=pltpu.SMEM)]
        + [pl.BlockSpec(memory_space=pltpu.HBM)] * 4,
        out_specs=[vmem] * 4,
        scratch_shapes=[whole] * 4
        + [flat] * 4
        + [by_head] * 4
        + [pltpu.VMEM((rows, rows), jnp.float32), square, square, squares, squares,
           pltpu.VMEM((2, heads, width, width), jnp.float32)]
        + [pltpu.SemaphoreType.DMA((4,)), pltpu.SemaphoreType.DMA((2, heads)), pltpu.SemaphoreType.DMA((2, heads))]
        + [pltpu.SemaphoreType.DMA((hops, heads))] * 4,
        compiler_params=pltpu.CompilerParams(
            collective_id=0, has_side_effects=True, vmem_limit_bytes=49 * 2**20
        ),
    )(doc_lengths, queries, keys, values, cotangent)


def solution(mesh):
    spec = P(("dp", "seq"), None, None)
    return jax.shard_map(
        functools.partial(local, mesh.shape["seq"]),
        mesh=mesh,
        in_specs=(spec, spec, spec, spec, P("dp")),
        out_specs=(spec, spec, spec, spec),
        check_vma=False,
    )
```

```python
import functools

import jax
import jax.numpy as jnp
from jax import lax
from jax.experimental import pallas as pl
from jax.experimental.pallas import tpu as pltpu
from jax.sharding import PartitionSpec as P

BLOCK = 256
LONGEST_PART = 4
MESH = pl.DeviceIdType.MESH
INNER_LAG, OUTER_LAG = 3, 5
LOAD_PARTS, STORE_PARTS = 4, 4


def dot(a, b, ca, cb):
    return lax.dot_general(
        a, b, (((ca,), (cb,)), ((), ())), preferred_element_type=jnp.float32
    )


def kernel(
    seq, hops,
    lengths, q_hbm, k_hbm, v_hbm, c_hbm,
    att_out, gq_out, gk_out, gv_out,
    q_in, k_in, v_in, c_in, qf, kf, vf, cf, qh, kh, vh, ch,
    mask, state, ret, state_in, ret_in, relay_in,
    load_sem, relay_send, relay_recv, state_send, state_recv, ret_send, ret_recv,
):
    rows, heads, width = q_in.shape
    loads = [
        pltpu.make_async_copy(src, dst, load_sem.at[i])
        for i, (src, dst) in enumerate(
            ((k_hbm, k_in), (v_hbm, v_in), (q_hbm, q_in), (c_hbm, c_in))
        )
    ]
    for load in loads:
        load.start()
    factor = (width * BLOCK) ** (-0.5)
    dp, me = lax.axis_index("dp"), lax.axis_index("seq")
    first = me * rows
    last = first + rows - 1

    barrier = pltpu.get_barrier_semaphore()
    for d in range(1, hops + 1):
        for ok, peer in ((me + d < seq, me + d), (me - d >= 0, me - d)):
            @pl.when(ok)
            def _(peer=peer):
                pl.semaphore_signal(barrier, inc=1, device_id=(dp, peer), device_id_type=MESH)

    for d in range(hops):
        @pl.when(me - d - 1 < 0)
        def _(d=d):
            state_in[d] = jnp.zeros(state_in.shape[1:], state_in.dtype)

        @pl.when(me + d + 1 >= seq)
        def _(d=d):
            ret_in[d] = jnp.zeros(ret_in.shape[1:], ret_in.dtype)

    big = jnp.int32(2**30)
    zero = jnp.int32(0)
    ends = []
    total = zero
    for j in range(lengths.shape[0]):
        total = total + lengths[j]
        ends.append(total)

    def start_of(p):
        out = zero
        for e in ends:
            out = jnp.maximum(out, jnp.where(e <= p, e, zero))
        return out

    def end_of(p):
        out = big
        for e in ends:
            out = jnp.minimum(out, jnp.where(e > p, e, big))
        return out

    tail_start = start_of(last + 1)
    head_end_prev = end_of(first - 1)
    head_start, head_end = start_of(first), end_of(first)
    last_start, last_end = start_of(last), end_of(last)

    step = 16

    def widen(*pairs):
        def part(i, _):
            at = pl.multiple_of(i * step, step)
            for src, dst in pairs:
                block = src[pl.ds(at, step)].astype(jnp.float32)
                dst[pl.ds(at * heads, step * heads), :] = block.reshape(step * heads, width)
            return 0

        lax.fori_loop(0, rows // step, part, 0)

    pl.semaphore_wait(barrier, jnp.minimum(me, hops) + jnp.minimum(seq - 1 - me, hops))

    pos = first + lax.broadcasted_iota(jnp.int32, (rows, width), 0)
    in_tail = pos >= tail_start
    in_head = pos < head_end_prev

    def forward(d, h):
        return pltpu.make_async_remote_copy(
            src_ref=state.at[h], dst_ref=state_in.at[d, h],
            send_sem=state_send.at[d, h], recv_sem=state_recv.at[d, h],
            device_id=(dp, me + d + 1), device_id_type=MESH,
        )

    def backward(d, h):
        return pltpu.make_async_remote_copy(
            src_ref=ret.at[h], dst_ref=ret_in.at[d, h],
            send_sem=ret_send.at[d, h], recv_sem=ret_recv.at[d, h],
            device_id=(dp, me - d - 1), device_id_type=MESH,
        )

    levels = max(seq // 2, 1)
    odd = lax.rem(me, 2) == 1
    even = lax.rem(me, 2) == 0
    level = me // 2
    up, down = me + 1 < seq, me >= 1

    def state_turn(h):
        return lax.rem(h, levels) < levels - 1 - level

    def ret_turn(h):
        return lax.rem(h, levels) < level

    def state_via(h):
        return odd & up & state_turn(h)

    def state_relays(h):
        return even & (me + 2 < seq) & state_turn(h)

    def ret_via(h):
        return even & (me >= 2) & up & ret_turn(h)

    def ret_relays(h):
        return odd & (me >= 2) & ret_turn(h)

    def via_state(h):
        return pltpu.make_async_remote_copy(
            src_ref=state.at[h], dst_ref=relay_in.at[0, h],
            send_sem=state_send.at[0, h], recv_sem=relay_recv.at[0, h],
            device_id=(dp, me - 1), device_id_type=MESH,
        )

    def via_ret(h):
        return pltpu.make_async_remote_copy(
            src_ref=ret.at[h], dst_ref=relay_in.at[1, h],
            send_sem=ret_send.at[0, h], recv_sem=relay_recv.at[1, h],
            device_id=(dp, me + 1), device_id_type=MESH,
        )

    def relay_state(h):
        return pltpu.make_async_remote_copy(
            src_ref=relay_in.at[0, h], dst_ref=state_in.at[0, h],
            send_sem=relay_send.at[0, h], recv_sem=state_recv.at[0, h],
            device_id=(dp, me + 2), device_id_type=MESH,
        )

    def relay_ret(h):
        return pltpu.make_async_remote_copy(
            src_ref=relay_in.at[1, h], dst_ref=ret_in.at[0, h],
            send_sem=relay_send.at[1, h], recv_sem=ret_recv.at[0, h],
            device_id=(dp, me - 2), device_id_type=MESH,
        )

    def sends_state(d, h):
        if d == 0 and hops > 1:
            return up & jnp.logical_not(state_via(h))
        return me + d + 1 < seq

    def sends_ret(d, h):
        if d == 0 and hops > 1:
            return down & jnp.logical_not(ret_via(h))
        return me - d - 1 >= 0

    def arrived_state(h):
        return pltpu.make_async_remote_copy(
            src_ref=state.at[h], dst_ref=relay_in.at[0, h],
            send_sem=state_send.at[0, h], recv_sem=relay_recv.at[0, h],
            device_id=(dp, me + 1), device_id_type=MESH,
        )

    def arrived_ret(h):
        return pltpu.make_async_remote_copy(
            src_ref=ret.at[h], dst_ref=relay_in.at[1, h],
            send_sem=ret_send.at[0, h], recv_sem=relay_recv.at[1, h],
            device_id=(dp, me - 1), device_id_type=MESH,
        )

    def relay(h):
        if hops > 1:
            @pl.when(state_relays(h))
            def _():
                arrived_state(h).wait_recv()
                relay_state(h).start()

            @pl.when(ret_relays(h))
            def _():
                arrived_ret(h).wait_recv()
                relay_ret(h).start()

    def state_sum(h):
        k32 = kf[pl.ds(h, rows, stride=heads), :]
        v16 = vf[pl.ds(h, rows, stride=heads), :].astype(jnp.bfloat16)
        kh[h] = k32.astype(jnp.bfloat16)
        vh[h] = v16
        state[h] = dot(jnp.where(in_tail, k32, 0.0).astype(jnp.bfloat16), v16, 0, 0)
        if hops > 1:
            @pl.when(state_via(h))
            def _():
                via_state(h).start()

        for d in range(hops):
            @pl.when(sends_state(d, h))
            def _(d=d):
                forward(d, h).start()

    def ret_sum(h):
        q32 = qf[pl.ds(h, rows, stride=heads), :]
        c16 = cf[pl.ds(h, rows, stride=heads), :].astype(jnp.bfloat16)
        qh[h] = q32.astype(jnp.bfloat16)
        ch[h] = c16
        ret[h] = dot(jnp.where(in_head, q32, 0.0).astype(jnp.bfloat16), c16, 0, 0)
        if hops > 1:
            @pl.when(ret_via(h))
            def _():
                via_ret(h).start()

        for d in range(hops):
            @pl.when(sends_ret(d, h))
            def _(d=d):
                backward(d, h).start()

    def each(fn):
        def body(h, _):
            fn(h)
            return 0

        return body

    ahead = min(4, heads)
    loads[0].wait()
    loads[1].wait()
    widen((k_in, kf), (v_in, vf))
    lax.fori_loop(0, ahead, each(state_sum), 0)
    loads[2].wait()
    loads[3].wait()
    widen((q_in, qf), (c_in, cf))

    def both(h):
        ret_sum(h)
        state_sum(h + ahead)

    lax.fori_loop(0, heads - ahead, each(both), 0)
    lax.fori_loop(heads - ahead, heads, each(ret_sum), 0)

    t_pos = first + lax.broadcasted_iota(jnp.int32, (rows, rows), 0)
    s_pos = first + lax.broadcasted_iota(jnp.int32, (rows, rows), 1)
    col = first + lax.broadcasted_iota(jnp.int32, (rows, 1), 0)
    begin = jnp.zeros((rows, 1), jnp.int32)
    for e in ends:
        begin = jnp.maximum(begin, jnp.where(col >= e, e, 0))
    visible = (s_pos <= t_pos) & (s_pos >= begin)
    mask[...] = jnp.where(visible, factor, 0.0).astype(jnp.float32)

    lead = heads // 8

    def inside(h, _):
        @pl.when(h >= heads // 2 - lead)
        def _():
            relay(h - (heads // 2 - lead))

        q, k, v, c = qh[h], kh[h], vh[h], ch[h]
        m = mask[...]
        weights = (m * dot(q, k, 1, 1)).astype(jnp.bfloat16)
        grad_weights = (m * dot(c, v, 1, 1)).astype(jnp.bfloat16)
        spot = pl.ds(h, rows, stride=heads)
        qf[spot, :] = dot(weights, v, 1, 0)
        kf[spot, :] = dot(grad_weights, k, 1, 0)
        vf[spot, :] = dot(grad_weights, q, 0, 0)
        cf[spot, :] = dot(weights, c, 0, 0)
        return 0

    lax.fori_loop(0, heads, inside, 0)

    head_factor = jnp.where(pos < head_end, factor, 0.0).astype(jnp.float32)
    tail_factor = jnp.where(pos >= last_start, factor, 0.0).astype(jnp.float32)

    def outside(h, _):
        carried = jnp.zeros((width, width), jnp.float32)
        returned = jnp.zeros((width, width), jnp.float32)
        @pl.when((h >= heads - heads // 2) & (h + lead < heads))
        def _():
            relay(h + lead)

        for d in range(hops):
            @pl.when(me - d - 1 >= 0)
            def _(d=d):
                forward(d, h).wait_recv()

            @pl.when(me + d + 1 < seq)
            def _(d=d):
                backward(d, h).wait_recv()

            here = head_start <= first - d * rows
            carried = carried + jnp.where(here, state_in[d, h], 0.0)
            there = last_end >= last + d * rows + 1
            returned = returned + jnp.where(there, ret_in[d, h], 0.0)
        carried = carried.astype(jnp.bfloat16)
        returned = returned.astype(jnp.bfloat16)
        q, k, v, c = qh[h], kh[h], vh[h], ch[h]
        spot = pl.ds(h, rows, stride=heads)
        qf[spot, :] = qf[spot, :] + head_factor * dot(q, carried, 1, 0)
        kf[spot, :] = kf[spot, :] + head_factor * dot(c, carried, 1, 1)
        vf[spot, :] = vf[spot, :] + tail_factor * dot(v, returned, 1, 1)
        cf[spot, :] = cf[spot, :] + tail_factor * dot(k, returned, 1, 0)
        return 0

    lax.fori_loop(0, heads, outside, 0)

    def narrow(i, _):
        at = pl.multiple_of(i * step, step)
        for src, dst in ((qf, att_out), (kf, gq_out), (vf, gk_out), (cf, gv_out)):
            block = src[pl.ds(at * heads, step * heads), :].reshape(step, heads, width)
            dst[pl.ds(at, step)] = block.astype(jnp.bfloat16)
        return 0

    lax.fori_loop(0, rows // step, narrow, 0)

    def drain(h):
        for d in range(hops):
            @pl.when(sends_state(d, h))
            def _(d=d):
                forward(d, h).wait_send()

            @pl.when(sends_ret(d, h))
            def _(d=d):
                backward(d, h).wait_send()

        if hops > 1:
            @pl.when(state_via(h))
            def _():
                via_state(h).wait_send()

            @pl.when(ret_via(h))
            def _():
                via_ret(h).wait_send()

            @pl.when(state_relays(h))
            def _():
                relay_state(h).wait_send()

            @pl.when(ret_relays(h))
            def _():
                relay_ret(h).wait_send()

    lax.fori_loop(0, heads, each(drain), 0)


def paired(
    seq,
    lens_hbm, q_hbm, k_hbm, v_hbm, c_hbm,
    o1, o2, o3, o4,
    lengths, xa_in, xb_in, pa_in, pb_in, xa_h, xb_h, pa_h, pb_h,
    mask, x_rows, p_rows, x_scale, p_scale,
    x_out, p_raw, p_sum, near_in, far_in, pair_in, relay_in, relay_sum,
    len_sem, load_sem, near_send, near_recv, far_send, far_recv,
    pair_send, pair_recv, relay_send, relay_recv,
):
    rows, heads, width = xa_in.shape
    factor = (width * BLOCK) ** (-0.5)
    dp, me = lax.axis_index("dp"), lax.axis_index("seq")
    odd = lax.rem(me, 2) == 1
    even = jnp.logical_not(odd)
    toward = jnp.where(odd, 1, -1)
    first = me * rows
    last = first + rows - 1
    parts = load_sem.shape[1]
    span = rows // parts

    len_load = pltpu.make_async_copy(lens_hbm, lengths, len_sem)
    len_load.start()

    def load(i, part, src, dst):
        cut = pl.ds(part * span, span)
        return pltpu.make_async_copy(src.at[cut], dst.at[cut], load_sem.at[i, part])

    landing = (xa_in, xb_in, pa_in, pb_in)

    @pl.when(even)
    def _():
        for pair in (0, 2):
            for part in range(parts):
                for i in (pair, pair + 1):
                    load(i, part, (q_hbm, c_hbm, k_hbm, v_hbm)[i], landing[i]).start()

    @pl.when(odd)
    def _():
        for pair in (0, 2):
            for part in range(parts):
                for i in (pair, pair + 1):
                    load(i, part, (k_hbm, v_hbm, q_hbm, c_hbm)[i], landing[i]).start()

    near, pair = me + toward, me - toward
    far_to, far_from = me - 2 * toward, me + 2 * toward
    near_ok = (near >= 0) & (near < seq)
    far_to_ok = (far_to >= 0) & (far_to < seq)
    far_from_ok = (far_from >= 0) & (far_from < seq)

    barrier = pltpu.get_barrier_semaphore()
    for ok, peer in ((near_ok, near), (pair >= 0, pair), (far_to_ok, far_to), (far_from_ok, far_from)):
        @pl.when(ok)
        def _(peer=peer):
            pl.semaphore_signal(barrier, inc=1, device_id=(dp, peer), device_id_type=MESH)

    @pl.when(jnp.logical_not(near_ok))
    def _():
        near_in[...] = jnp.zeros(near_in.shape, near_in.dtype)

    @pl.when(jnp.logical_not(far_from_ok))
    def _():
        far_in[...] = jnp.zeros(far_in.shape, far_in.dtype)

    len_load.wait()
    big = jnp.int32(2**30)
    zero = jnp.int32(0)
    ends = []
    total = zero
    for j in range(lengths.shape[0]):
        total = total + lengths[j]
        ends.append(total)

    def start_of(p):
        out = zero
        for e in ends:
            out = jnp.maximum(out, jnp.where(e <= p, e, zero))
        return out

    def end_of(p):
        out = big
        for e in ends:
            out = jnp.minimum(out, jnp.where(e > p, e, big))
        return out

    tail_start = start_of(last + 1)
    head_end_prev = end_of(first - 1)
    head_start, head_end = start_of(first), end_of(first)
    last_start, last_end = start_of(last), end_of(last)
    x_keep = jnp.where(odd, last_end >= last + rows + 1, head_start <= first - rows)
    p_keep = jnp.where(odd, head_end_prev >= last + 1, tail_start <= first)
    relay_keep = jnp.where(odd, end_of(first - rows - 1) >= first, start_of(last + rows + 1) <= last + 1)

    pos = first + lax.broadcasted_iota(jnp.int32, (rows, width), 0)
    x_low, x_high = jnp.where(odd, tail_start, zero), jnp.where(odd, big, head_end_prev)
    p_low, p_high = jnp.where(odd, zero, tail_start), jnp.where(odd, head_end_prev, big)
    x_rows[...] = jnp.where((pos >= x_low) & (pos < x_high), 1.0, 0.0).astype(jnp.bfloat16)

    step = 16

    def widen(part, *pairs):
        def some(i, _):
            at = pl.multiple_of(part * span + i * step, step)
            for src, dst in pairs:
                block = src[pl.ds(at, step)].astype(jnp.float32)
                dst[pl.ds(at * heads, step * heads), :] = block.reshape(step * heads, width)
            return 0

        lax.fori_loop(0, span // step, some, 0)

    levels = seq // 2
    level = me // 2
    mine = jnp.where(odd, levels - 1 - level, level)
    theirs = levels - 1 - mine

    def my_turn(h):
        return lax.rem(h, levels) < mine

    def their_turn(h):
        return lax.rem(h, levels) < theirs

    def near_turn(h):
        return lax.rem(h, levels) < jnp.where(odd, level + 1, levels - level)

    def remote(src, dst, send, recv, peer):
        return pltpu.make_async_remote_copy(
            src_ref=src, dst_ref=dst, send_sem=send, recv_sem=recv,
            device_id=(dp, peer), device_id_type=MESH,
        )

    def direct(h):
        return remote(x_out.at[h], near_in.at[h], near_send.at[h], near_recv.at[h], near)

    def via(h):
        return remote(x_out.at[h], relay_in.at[h], near_send.at[h], relay_recv.at[h], pair)

    def onward(h):
        return remote(relay_sum.at[h], near_in.at[h], relay_send.at[h], near_recv.at[h], far_to)

    def far(h):
        return remote(p_raw.at[h], far_in.at[h], far_send.at[h], far_recv.at[h], far_to)

    def across(h):
        return remote(p_sum.at[h], pair_in.at[h], pair_send.at[h], pair_recv.at[h], pair)

    for part in range(parts):
        for i in (0, 1):
            load(i, part, q_hbm, landing[i]).wait()
        widen(part, (xa_in, o1), (xb_in, o2))

    pl.semaphore_wait(
        barrier, 1 + near_ok.astype(jnp.int32) + far_to_ok.astype(jnp.int32) + far_from_ok.astype(jnp.int32)
    )

    def x_state(h, _):
        spot = pl.ds(h, rows, stride=heads)
        xa = o1[spot, :].astype(jnp.bfloat16)
        xb = o2[spot, :].astype(jnp.bfloat16)
        xa_h[h] = xa
        xb_h[h] = xb
        x_out[h] = dot(xa * x_rows[...], xb, 0, 0)

        @pl.when(my_turn(h))
        def _():
            via(h).start()

        @pl.when(near_ok & jnp.logical_not(my_turn(h)))
        def _():
            direct(h).start()

        return 0

    lax.fori_loop(0, heads, x_state, 0)

    p_rows[...] = jnp.where((pos >= p_low) & (pos < p_high), 1.0, 0.0).astype(jnp.bfloat16)
    in_head, in_tail = pos < head_end, pos >= last_start
    head_scale = jnp.where(in_head, factor, 0.0).astype(jnp.float32)
    tail_scale = jnp.where(in_tail, factor, 0.0).astype(jnp.float32)
    x_scale[...] = jnp.where(odd, tail_scale, head_scale)
    p_scale[...] = jnp.where(odd, head_scale, tail_scale)
    col = first + lax.broadcasted_iota(jnp.int32, (1, rows), 1)
    begin = jnp.zeros((1, rows), jnp.int32)
    finish = jnp.full((1, rows), big, jnp.int32)
    for e in ends:
        begin = jnp.maximum(begin, jnp.where(col >= e, e, zero))
        finish = jnp.minimum(finish, jnp.where(col < e, e, big))
    low, high = jnp.where(odd, begin, col), jnp.where(odd, col + 1, finish)
    row = first + lax.broadcasted_iota(jnp.int32, (rows, rows), 0)
    mask[...] = jnp.where((row >= low) & (row < high), factor, 0.0).astype(jnp.float32)

    for part in range(parts):
        for i in (2, 3):
            load(i, part, q_hbm, landing[i]).wait()
        widen(part, (pa_in, o3), (pb_in, o4))

    def p_state(h):
        spot = pl.ds(h, rows, stride=heads)
        pa = o3[spot, :].astype(jnp.bfloat16)
        pb = o4[spot, :].astype(jnp.bfloat16)
        pa_h[h] = pa
        pb_h[h] = pb
        p_raw[h] = dot(pa * p_rows[...], pb, 0, 0)

        @pl.when(far_to_ok & jnp.logical_not(their_turn(h)))
        def _():
            far(h).start()

    def relay(h):
        @pl.when(their_turn(h))
        def _():
            remote(x_out.at[h], relay_in.at[h], near_send.at[h], relay_recv.at[h], pair).wait_recv()
            relay_sum[h] = relay_in[h] + jnp.where(relay_keep, p_raw[h], 0.0)
            onward(h).start()

    def inner(h):
        @pl.when(near_ok)
        def _():
            direct(h).wait_recv()

        p_sum[h] = p_raw[h] + jnp.where(p_keep, near_in[h], 0.0)
        across(h).start()

        @pl.when(far_from_ok & jnp.logical_not(near_turn(h)))
        def _():
            far(h).wait_recv()

        close = (near_in[h] + jnp.where(x_keep & jnp.logical_not(near_turn(h)), far_in[h], 0.0)).astype(jnp.bfloat16)
        xa, xb, pa, pb = xa_h[h], xb_h[h], pa_h[h], pb_h[h]
        m = mask[...]
        w1 = (m * dot(xa, pa, 1, 1)).astype(jnp.bfloat16)
        w2 = (m * dot(xb, pb, 1, 1)).astype(jnp.bfloat16)
        spot = pl.ds(h, rows, stride=heads)
        scale = x_scale[...]
        o1[spot, :] = dot(w1, pb, 1, 0) + scale * dot(xa, close, 1, 0)
        o2[spot, :] = dot(w2, pa, 1, 0) + scale * dot(xb, close, 1, 1)
        o3[spot, :] = dot(w2, xa, 0, 0)
        o4[spot, :] = dot(w1, xb, 0, 0)

    def outer(h):
        across(h).wait_recv()
        other = pair_in[h].astype(jnp.bfloat16)
        pa, pb = pa_h[h], pb_h[h]
        spot = pl.ds(h, rows, stride=heads)
        scale = p_scale[...]
        o3[spot, :] = o3[spot, :] + scale * dot(pb, other, 1, 1)
        o4[spot, :] = o4[spot, :] + scale * dot(pa, other, 1, 0)

    inner_lag, outer_lag = INNER_LAG, OUTER_LAG

    def turn(i, _):
        @pl.when(i < heads)
        def _():
            p_state(i)
            relay(i)

        @pl.when((i >= inner_lag) & (i < heads + inner_lag))
        def _():
            inner(i - inner_lag)

        @pl.when(i >= outer_lag)
        def _():
            outer(i - outer_lag)

        return 0

    lax.fori_loop(0, heads + outer_lag, turn, 0)

    def drain(h, _):
        across(h).wait_send()

        @pl.when(near_ok)
        def _():
            direct(h).wait_send()

        @pl.when(far_to_ok & jnp.logical_not(their_turn(h)))
        def _():
            far(h).wait_send()

        @pl.when(their_turn(h))
        def _():
            onward(h).wait_send()

        return 0

    lax.fori_loop(0, heads, drain, 0)


def settle(i1, i2, i3, i4, att, gq, gk, gv, s1, s2, s3, s4, sem):
    rows, heads, width = s1.shape
    parts = sem.shape[1]
    span = rows // parts
    step = 16
    odd = lax.rem(lax.axis_index("seq"), 2) == 1
    stages = (s1, s2, s3, s4)
    forward, reverse = (att, gq, gk, gv), (gv, gk, gq, att)

    def put(i, part, dst):
        cut = pl.ds(part * span, span)
        return pltpu.make_async_copy(stages[i].at[cut], dst.at[cut], sem.at[i, part])

    for part in range(parts):
        def narrow(i, _):
            at = pl.multiple_of(part * span + i * step, step)
            for src, dst in zip((i1, i2, i3, i4), stages):
                block = src[pl.ds(at * heads, step * heads), :].reshape(step, heads, width)
                dst[pl.ds(at, step)] = block.astype(jnp.bfloat16)
            return 0

        lax.fori_loop(0, span // step, narrow, 0)

        @pl.when(odd)
        def _():
            for i in range(4):
                put(i, part, reverse[i]).start()

        @pl.when(jnp.logical_not(odd))
        def _():
            for i in range(4):
                put(i, part, forward[i]).start()

    for part in range(parts):
        for i in range(4):
            put(i, part, att).wait()


def local_paired(seq, queries, keys, values, cotangent, doc_lengths):
    rows, heads, width = queries.shape
    vmem = pl.BlockSpec(memory_space=pltpu.VMEM)
    hbm = pl.BlockSpec(memory_space=pltpu.HBM)
    whole = pltpu.VMEM((rows, heads, width), jnp.bfloat16)
    by_head = pltpu.VMEM((heads, rows, width), jnp.bfloat16)
    square = pltpu.VMEM((heads, width, width), jnp.float32)
    flat = jax.ShapeDtypeStruct((rows * heads, width), jnp.float32)
    each = pltpu.SemaphoreType.DMA((heads,))
    held = pl.pallas_call(
        functools.partial(paired, seq),
        out_shape=[flat] * 4,
        in_specs=[hbm] * 5,
        out_specs=[vmem] * 4,
        scratch_shapes=[pltpu.SMEM(doc_lengths.shape, jnp.int32)]
        + [whole] * 4
        + [by_head] * 4
        + [pltpu.VMEM((rows, rows), jnp.float32)]
        + [pltpu.VMEM((rows, width), jnp.bfloat16)] * 2
        + [pltpu.VMEM((rows, width), jnp.float32)] * 2
        + [square] * 8
        + [pltpu.SemaphoreType.DMA, pltpu.SemaphoreType.DMA((4, LOAD_PARTS))]
        + [each] * 8,
        compiler_params=pltpu.CompilerParams(
            collective_id=0, has_side_effects=True, vmem_limit_bytes=40 * 2**20
        ),
    )(*(pltpu.with_memory_space_constraint(a, pltpu.HBM) for a in (doc_lengths, queries, keys, values, cotangent)))
    return pl.pallas_call(
        settle,
        out_shape=[jax.ShapeDtypeStruct(queries.shape, jnp.bfloat16)] * 4,
        in_specs=[vmem] * 4,
        out_specs=[hbm] * 4,
        scratch_shapes=[whole] * 4 + [pltpu.SemaphoreType.DMA((4, STORE_PARTS))],
        compiler_params=pltpu.CompilerParams(vmem_limit_bytes=24 * 2**20),
    )(*held)


def local(seq, queries, keys, values, cotangent, doc_lengths):
    rows, heads, width = queries.shape
    longest = seq * rows // LONGEST_PART
    hops = min(seq - 1, (longest - 1 + rows - 1) // rows)
    if hops == 2 and seq % 2 == 0:
        return local_paired(seq, queries, keys, values, cotangent, doc_lengths)
    vmem = pl.BlockSpec(memory_space=pltpu.VMEM)
    flat = pltpu.VMEM((rows * heads, width), jnp.float32)
    by_head = pltpu.VMEM((heads, rows, width), jnp.bfloat16)
    whole = pltpu.VMEM((rows, heads, width), jnp.bfloat16)
    square = pltpu.VMEM((heads, width, width), jnp.float32)
    squares = pltpu.VMEM((hops, heads, width, width), jnp.float32)
    return pl.pallas_call(
        functools.partial(kernel, seq, hops),
        out_shape=[jax.ShapeDtypeStruct(queries.shape, jnp.bfloat16)] * 4,
        in_specs=[pl.BlockSpec(memory_space=pltpu.SMEM)]
        + [pl.BlockSpec(memory_space=pltpu.HBM)] * 4,
        out_specs=[vmem] * 4,
        scratch_shapes=[whole] * 4
        + [flat] * 4
        + [by_head] * 4
        + [pltpu.VMEM((rows, rows), jnp.float32), square, square, squares, squares,
           pltpu.VMEM((2, heads, width, width), jnp.float32)]
        + [pltpu.SemaphoreType.DMA((4,)), pltpu.SemaphoreType.DMA((2, heads)), pltpu.SemaphoreType.DMA((2, heads))]
        + [pltpu.SemaphoreType.DMA((hops, heads))] * 4,
        compiler_params=pltpu.CompilerParams(
            collective_id=0, has_side_effects=True, vmem_limit_bytes=49 * 2**20
        ),
    )(doc_lengths, queries, keys, values, cotangent)


def solution(mesh):
    spec = P(("dp", "seq"), None, None)
    return jax.shard_map(
        functools.partial(local, mesh.shape["seq"]),
        mesh=mesh,
        in_specs=(spec, spec, spec, spec, P("dp")),
        out_specs=(spec, spec, spec, spec),
        check_vma=False,
    )
```

```python
import functools

import jax
import jax.numpy as jnp
from jax import lax
from jax.experimental import pallas as pl
from jax.experimental.pallas import tpu as pltpu
from jax.sharding import PartitionSpec as P

BLOCK = 256
LONGEST_PART = 4
MESH = pl.DeviceIdType.MESH
INNER_LAG, OUTER_LAG = 6, 9
LOAD_PARTS, STORE_PARTS = 2, 4


def dot(a, b, ca, cb):
    return lax.dot_general(
        a, b, (((ca,), (cb,)), ((), ())), preferred_element_type=jnp.float32
    )


def kernel(
    seq, hops,
    lengths, q_hbm, k_hbm, v_hbm, c_hbm,
    att_out, gq_out, gk_out, gv_out,
    q_in, k_in, v_in, c_in, qf, kf, vf, cf, qh, kh, vh, ch,
    mask, state, ret, state_in, ret_in, relay_in,
    load_sem, relay_send, relay_recv, state_send, state_recv, ret_send, ret_recv,
):
    rows, heads, width = q_in.shape
    loads = [
        pltpu.make_async_copy(src, dst, load_sem.at[i])
        for i, (src, dst) in enumerate(
            ((k_hbm, k_in), (v_hbm, v_in), (q_hbm, q_in), (c_hbm, c_in))
        )
    ]
    for load in loads:
        load.start()
    factor = (width * BLOCK) ** (-0.5)
    dp, me = lax.axis_index("dp"), lax.axis_index("seq")
    first = me * rows
    last = first + rows - 1

    barrier = pltpu.get_barrier_semaphore()
    for d in range(1, hops + 1):
        for ok, peer in ((me + d < seq, me + d), (me - d >= 0, me - d)):
            @pl.when(ok)
            def _(peer=peer):
                pl.semaphore_signal(barrier, inc=1, device_id=(dp, peer), device_id_type=MESH)

    for d in range(hops):
        @pl.when(me - d - 1 < 0)
        def _(d=d):
            state_in[d] = jnp.zeros(state_in.shape[1:], state_in.dtype)

        @pl.when(me + d + 1 >= seq)
        def _(d=d):
            ret_in[d] = jnp.zeros(ret_in.shape[1:], ret_in.dtype)

    big = jnp.int32(2**30)
    zero = jnp.int32(0)
    ends = []
    total = zero
    for j in range(lengths.shape[0]):
        total = total + lengths[j]
        ends.append(total)

    def start_of(p):
        out = zero
        for e in ends:
            out = jnp.maximum(out, jnp.where(e <= p, e, zero))
        return out

    def end_of(p):
        out = big
        for e in ends:
            out = jnp.minimum(out, jnp.where(e > p, e, big))
        return out

    tail_start = start_of(last + 1)
    head_end_prev = end_of(first - 1)
    head_start, head_end = start_of(first), end_of(first)
    last_start, last_end = start_of(last), end_of(last)

    step = 16

    def widen(*pairs):
        def part(i, _):
            at = pl.multiple_of(i * step, step)
            for src, dst in pairs:
                block = src[pl.ds(at, step)].astype(jnp.float32)
                dst[pl.ds(at * heads, step * heads), :] = block.reshape(step * heads, width)
            return 0

        lax.fori_loop(0, rows // step, part, 0)

    pl.semaphore_wait(barrier, jnp.minimum(me, hops) + jnp.minimum(seq - 1 - me, hops))

    pos = first + lax.broadcasted_iota(jnp.int32, (rows, width), 0)
    in_tail = pos >= tail_start
    in_head = pos < head_end_prev

    def forward(d, h):
        return pltpu.make_async_remote_copy(
            src_ref=state.at[h], dst_ref=state_in.at[d, h],
            send_sem=state_send.at[d, h], recv_sem=state_recv.at[d, h],
            device_id=(dp, me + d + 1), device_id_type=MESH,
        )

    def backward(d, h):
        return pltpu.make_async_remote_copy(
            src_ref=ret.at[h], dst_ref=ret_in.at[d, h],
            send_sem=ret_send.at[d, h], recv_sem=ret_recv.at[d, h],
            device_id=(dp, me - d - 1), device_id_type=MESH,
        )

    levels = max(seq // 2, 1)
    odd = lax.rem(me, 2) == 1
    even = lax.rem(me, 2) == 0
    level = me // 2
    up, down = me + 1 < seq, me >= 1

    def state_turn(h):
        return lax.rem(h, levels) < levels - 1 - level

    def ret_turn(h):
        return lax.rem(h, levels) < level

    def state_via(h):
        return odd & up & state_turn(h)

    def state_relays(h):
        return even & (me + 2 < seq) & state_turn(h)

    def ret_via(h):
        return even & (me >= 2) & up & ret_turn(h)

    def ret_relays(h):
        return odd & (me >= 2) & ret_turn(h)

    def via_state(h):
        return pltpu.make_async_remote_copy(
            src_ref=state.at[h], dst_ref=relay_in.at[0, h],
            send_sem=state_send.at[0, h], recv_sem=relay_recv.at[0, h],
            device_id=(dp, me - 1), device_id_type=MESH,
        )

    def via_ret(h):
        return pltpu.make_async_remote_copy(
            src_ref=ret.at[h], dst_ref=relay_in.at[1, h],
            send_sem=ret_send.at[0, h], recv_sem=relay_recv.at[1, h],
            device_id=(dp, me + 1), device_id_type=MESH,
        )

    def relay_state(h):
        return pltpu.make_async_remote_copy(
            src_ref=relay_in.at[0, h], dst_ref=state_in.at[0, h],
            send_sem=relay_send.at[0, h], recv_sem=state_recv.at[0, h],
            device_id=(dp, me + 2), device_id_type=MESH,
        )

    def relay_ret(h):
        return pltpu.make_async_remote_copy(
            src_ref=relay_in.at[1, h], dst_ref=ret_in.at[0, h],
            send_sem=relay_send.at[1, h], recv_sem=ret_recv.at[0, h],
            device_id=(dp, me - 2), device_id_type=MESH,
        )

    def sends_state(d, h):
        if d == 0 and hops > 1:
            return up & jnp.logical_not(state_via(h))
        return me + d + 1 < seq

    def sends_ret(d, h):
        if d == 0 and hops > 1:
            return down & jnp.logical_not(ret_via(h))
        return me - d - 1 >= 0

    def arrived_state(h):
        return pltpu.make_async_remote_copy(
            src_ref=state.at[h], dst_ref=relay_in.at[0, h],
            send_sem=state_send.at[0, h], recv_sem=relay_recv.at[0, h],
            device_id=(dp, me + 1), device_id_type=MESH,
        )

    def arrived_ret(h):
        return pltpu.make_async_remote_copy(
            src_ref=ret.at[h], dst_ref=relay_in.at[1, h],
            send_sem=ret_send.at[0, h], recv_sem=relay_recv.at[1, h],
            device_id=(dp, me - 1), device_id_type=MESH,
        )

    def relay(h):
        if hops > 1:
            @pl.when(state_relays(h))
            def _():
                arrived_state(h).wait_recv()
                relay_state(h).start()

            @pl.when(ret_relays(h))
            def _():
                arrived_ret(h).wait_recv()
                relay_ret(h).start()

    def state_sum(h):
        k32 = kf[pl.ds(h, rows, stride=heads), :]
        v16 = vf[pl.ds(h, rows, stride=heads), :].astype(jnp.bfloat16)
        kh[h] = k32.astype(jnp.bfloat16)
        vh[h] = v16
        state[h] = dot(jnp.where(in_tail, k32, 0.0).astype(jnp.bfloat16), v16, 0, 0)
        if hops > 1:
            @pl.when(state_via(h))
            def _():
                via_state(h).start()

        for d in range(hops):
            @pl.when(sends_state(d, h))
            def _(d=d):
                forward(d, h).start()

    def ret_sum(h):
        q32 = qf[pl.ds(h, rows, stride=heads), :]
        c16 = cf[pl.ds(h, rows, stride=heads), :].astype(jnp.bfloat16)
        qh[h] = q32.astype(jnp.bfloat16)
        ch[h] = c16
        ret[h] = dot(jnp.where(in_head, q32, 0.0).astype(jnp.bfloat16), c16, 0, 0)
        if hops > 1:
            @pl.when(ret_via(h))
            def _():
                via_ret(h).start()

        for d in range(hops):
            @pl.when(sends_ret(d, h))
            def _(d=d):
                backward(d, h).start()

    def each(fn):
        def body(h, _):
            fn(h)
            return 0

        return body

    ahead = min(4, heads)
    loads[0].wait()
    loads[1].wait()
    widen((k_in, kf), (v_in, vf))
    lax.fori_loop(0, ahead, each(state_sum), 0)
    loads[2].wait()
    loads[3].wait()
    widen((q_in, qf), (c_in, cf))

    def both(h):
        ret_sum(h)
        state_sum(h + ahead)

    lax.fori_loop(0, heads - ahead, each(both), 0)
    lax.fori_loop(heads - ahead, heads, each(ret_sum), 0)

    t_pos = first + lax.broadcasted_iota(jnp.int32, (rows, rows), 0)
    s_pos = first + lax.broadcasted_iota(jnp.int32, (rows, rows), 1)
    col = first + lax.broadcasted_iota(jnp.int32, (rows, 1), 0)
    begin = jnp.zeros((rows, 1), jnp.int32)
    for e in ends:
        begin = jnp.maximum(begin, jnp.where(col >= e, e, 0))
    visible = (s_pos <= t_pos) & (s_pos >= begin)
    mask[...] = jnp.where(visible, factor, 0.0).astype(jnp.float32)

    lead = heads // 8

    def inside(h, _):
        @pl.when(h >= heads // 2 - lead)
        def _():
            relay(h - (heads // 2 - lead))

        q, k, v, c = qh[h], kh[h], vh[h], ch[h]
        m = mask[...]
        weights = (m * dot(q, k, 1, 1)).astype(jnp.bfloat16)
        grad_weights = (m * dot(c, v, 1, 1)).astype(jnp.bfloat16)
        spot = pl.ds(h, rows, stride=heads)
        qf[spot, :] = dot(weights, v, 1, 0)
        kf[spot, :] = dot(grad_weights, k, 1, 0)
        vf[spot, :] = dot(grad_weights, q, 0, 0)
        cf[spot, :] = dot(weights, c, 0, 0)
        return 0

    lax.fori_loop(0, heads, inside, 0)

    head_factor = jnp.where(pos < head_end, factor, 0.0).astype(jnp.float32)
    tail_factor = jnp.where(pos >= last_start, factor, 0.0).astype(jnp.float32)

    def outside(h, _):
        carried = jnp.zeros((width, width), jnp.float32)
        returned = jnp.zeros((width, width), jnp.float32)
        @pl.when((h >= heads - heads // 2) & (h + lead < heads))
        def _():
            relay(h + lead)

        for d in range(hops):
            @pl.when(me - d - 1 >= 0)
            def _(d=d):
                forward(d, h).wait_recv()

            @pl.when(me + d + 1 < seq)
            def _(d=d):
                backward(d, h).wait_recv()

            here = head_start <= first - d * rows
            carried = carried + jnp.where(here, state_in[d, h], 0.0)
            there = last_end >= last + d * rows + 1
            returned = returned + jnp.where(there, ret_in[d, h], 0.0)
        carried = carried.astype(jnp.bfloat16)
        returned = returned.astype(jnp.bfloat16)
        q, k, v, c = qh[h], kh[h], vh[h], ch[h]
        spot = pl.ds(h, rows, stride=heads)
        qf[spot, :] = qf[spot, :] + head_factor * dot(q, carried, 1, 0)
        kf[spot, :] = kf[spot, :] + head_factor * dot(c, carried, 1, 1)
        vf[spot, :] = vf[spot, :] + tail_factor * dot(v, returned, 1, 1)
        cf[spot, :] = cf[spot, :] + tail_factor * dot(k, returned, 1, 0)
        return 0

    lax.fori_loop(0, heads, outside, 0)

    def narrow(i, _):
        at = pl.multiple_of(i * step, step)
        for src, dst in ((qf, att_out), (kf, gq_out), (vf, gk_out), (cf, gv_out)):
            block = src[pl.ds(at * heads, step * heads), :].reshape(step, heads, width)
            dst[pl.ds(at, step)] = block.astype(jnp.bfloat16)
        return 0

    lax.fori_loop(0, rows // step, narrow, 0)

    def drain(h):
        for d in range(hops):
            @pl.when(sends_state(d, h))
            def _(d=d):
                forward(d, h).wait_send()

            @pl.when(sends_ret(d, h))
            def _(d=d):
                backward(d, h).wait_send()

        if hops > 1:
            @pl.when(state_via(h))
            def _():
                via_state(h).wait_send()

            @pl.when(ret_via(h))
            def _():
                via_ret(h).wait_send()

            @pl.when(state_relays(h))
            def _():
                relay_state(h).wait_send()

            @pl.when(ret_relays(h))
            def _():
                relay_ret(h).wait_send()

    lax.fori_loop(0, heads, each(drain), 0)


def paired(
    seq,
    lens_hbm, q_hbm, k_hbm, v_hbm, c_hbm,
    o1, o2, o3, o4,
    lengths, xa_in, xb_in, pa_in, pb_in, xa_h, xb_h, pa_h, pb_h,
    mask, x_rows, p_rows, x_scale, p_scale,
    x_out, p_raw, p_sum, near_in, far_in, pair_in, relay_in, relay_sum,
    len_sem, load_sem, near_send, far_send, pair_send,
    near_recv, far_recv, pair_recv, relay_recv,
):
    rows, heads, width = xa_in.shape
    factor = (width * BLOCK) ** (-0.5)
    dp, me = lax.axis_index("dp"), lax.axis_index("seq")
    odd = lax.rem(me, 2) == 1
    even = jnp.logical_not(odd)
    toward = jnp.where(odd, 1, -1)
    first = me * rows
    last = first + rows - 1
    near, pair = me + toward, me - toward
    far_to, far_from = me - 2 * toward, me + 2 * toward
    near_ok = (near >= 0) & (near < seq)
    far_to_ok = (far_to >= 0) & (far_to < seq)
    far_from_ok = (far_from >= 0) & (far_from < seq)

    barrier = pltpu.get_barrier_semaphore()
    for ok, peer in ((near_ok, near), (pair >= 0, pair), (far_to_ok, far_to), (far_from_ok, far_from)):
        @pl.when(ok)
        def _(peer=peer):
            pl.semaphore_signal(barrier, inc=1, device_id=(dp, peer), device_id_type=MESH)

    parts = load_sem.shape[1]
    span = rows // parts

    len_load = pltpu.make_async_copy(lens_hbm, lengths, len_sem)
    len_load.start()

    def load(i, part, src, dst):
        cut = pl.ds(part * span, span)
        return pltpu.make_async_copy(src.at[cut], dst.at[cut], load_sem.at[i, part])

    landing = (xa_in, xb_in, pa_in, pb_in)

    @pl.when(even)
    def _():
        for pair in (0, 2):
            for part in range(parts):
                for i in (pair, pair + 1):
                    load(i, part, (q_hbm, c_hbm, k_hbm, v_hbm)[i], landing[i]).start()

    @pl.when(odd)
    def _():
        for pair in (0, 2):
            for part in range(parts):
                for i in (pair, pair + 1):
                    load(i, part, (k_hbm, v_hbm, q_hbm, c_hbm)[i], landing[i]).start()

    len_load.wait()
    big = jnp.int32(2**30)
    zero = jnp.int32(0)
    ends = []
    total = zero
    for j in range(lengths.shape[0]):
        total = total + lengths[j]
        ends.append(total)

    def start_of(p):
        out = zero
        for e in ends:
            out = jnp.maximum(out, jnp.where(e <= p, e, zero))
        return out

    def end_of(p):
        out = big
        for e in ends:
            out = jnp.minimum(out, jnp.where(e > p, e, big))
        return out

    tail_start = start_of(last + 1)
    head_end_prev = end_of(first - 1)
    head_start, head_end = start_of(first), end_of(first)
    last_start, last_end = start_of(last), end_of(last)
    x_keep = jnp.where(odd, last_end >= last + rows + 1, head_start <= first - rows)
    p_keep = jnp.where(odd, head_end_prev >= last + 1, tail_start <= first)
    relay_keep = jnp.where(odd, end_of(first - rows - 1) >= first, start_of(last + rows + 1) <= last + 1)

    pos = first + lax.broadcasted_iota(jnp.int32, (rows, width), 0)
    x_low, x_high = jnp.where(odd, tail_start, zero), jnp.where(odd, big, head_end_prev)
    p_low, p_high = jnp.where(odd, zero, tail_start), jnp.where(odd, head_end_prev, big)
    x_rows[...] = jnp.where((pos >= x_low) & (pos < x_high), 1.0, 0.0).astype(jnp.bfloat16)

    step = 16

    def widen(part, *pairs):
        def some(i, _):
            at = pl.multiple_of(part * span + i * step, step)
            for src, dst in pairs:
                block = src[pl.ds(at, step)].astype(jnp.float32)
                dst[pl.ds(at * heads, step * heads), :] = block.reshape(step * heads, width)
            return 0

        lax.fori_loop(0, span // step, some, 0)

    levels = seq // 2
    level = me // 2
    mine = jnp.where(odd, levels - 1 - level, level)
    theirs = levels - 1 - mine

    def my_turn(h):
        return lax.rem(h, levels) < mine

    def their_turn(h):
        return lax.rem(h, levels) < theirs

    def near_turn(h):
        return lax.rem(h, levels) < jnp.where(odd, level + 1, levels - level)

    def remote(src, dst, send, recv, peer):
        return pltpu.make_async_remote_copy(
            src_ref=src, dst_ref=dst, send_sem=send, recv_sem=recv,
            device_id=(dp, peer), device_id_type=MESH,
        )

    def direct(h):
        return remote(x_out.at[h], near_in.at[h], near_send, near_recv.at[h], near)

    def via(h):
        return remote(x_out.at[h], relay_in.at[h], near_send, relay_recv.at[h], pair)

    def onward(h):
        return remote(relay_sum.at[h], near_in.at[h], far_send, near_recv.at[h], far_to)

    def far(h):
        return remote(p_raw.at[h], far_in.at[h], far_send, far_recv.at[h], far_to)

    def across(h):
        return remote(p_sum.at[h], pair_in.at[h], pair_send, pair_recv.at[h], pair)

    for part in range(parts):
        for i in (0, 1):
            load(i, part, q_hbm, landing[i]).wait()
        widen(part, (xa_in, o1), (xb_in, o2))

    pl.semaphore_wait(
        barrier, 1 + near_ok.astype(jnp.int32) + far_to_ok.astype(jnp.int32) + far_from_ok.astype(jnp.int32)
    )

    def x_state(h, _):
        spot = pl.ds(h, rows, stride=heads)
        xa = o1[spot, :].astype(jnp.bfloat16)
        xb = o2[spot, :].astype(jnp.bfloat16)
        xa_h[h] = xa
        xb_h[h] = xb

        @pl.when(near_ok)
        def _():
            x_out[h] = dot(xa * x_rows[...], xb, 0, 0)

        @pl.when(my_turn(h))
        def _():
            via(h).start()

        @pl.when(near_ok & jnp.logical_not(my_turn(h)))
        def _():
            direct(h).start()

        return 0

    lax.fori_loop(0, heads, x_state, 0)

    p_rows[...] = jnp.where((pos >= p_low) & (pos < p_high), 1.0, 0.0).astype(jnp.bfloat16)
    in_head, in_tail = pos < head_end, pos >= last_start
    head_scale = jnp.where(in_head, factor, 0.0).astype(jnp.float32)
    tail_scale = jnp.where(in_tail, factor, 0.0).astype(jnp.float32)
    x_scale[...] = jnp.where(odd, tail_scale, head_scale)
    p_scale[...] = jnp.where(odd, head_scale, tail_scale)
    col = first + lax.broadcasted_iota(jnp.int32, (1, rows), 1)
    begin = jnp.zeros((1, rows), jnp.int32)
    finish = jnp.full((1, rows), big, jnp.int32)
    for e in ends:
        begin = jnp.maximum(begin, jnp.where(col >= e, e, zero))
        finish = jnp.minimum(finish, jnp.where(col < e, e, big))
    low, high = jnp.where(odd, begin, col), jnp.where(odd, col + 1, finish)
    row = first + lax.broadcasted_iota(jnp.int32, (rows, rows), 0)
    mask[...] = jnp.where((row >= low) & (row < high), factor, 0.0).astype(jnp.float32)

    for part in range(parts):
        for i in (2, 3):
            load(i, part, q_hbm, landing[i]).wait()
        widen(part, (pa_in, o3), (pb_in, o4))

    def p_state(h):
        spot = pl.ds(h, rows, stride=heads)
        pa = o3[spot, :].astype(jnp.bfloat16)
        pb = o4[spot, :].astype(jnp.bfloat16)
        pa_h[h] = pa
        pb_h[h] = pb
        p_raw[h] = dot(pa * p_rows[...], pb, 0, 0)

        @pl.when(far_to_ok & jnp.logical_not(their_turn(h)))
        def _():
            far(h).start()

    def relay(h):
        @pl.when(their_turn(h))
        def _():
            remote(x_out.at[h], relay_in.at[h], near_send, relay_recv.at[h], pair).wait_recv()
            relay_sum[h] = relay_in[h] + jnp.where(relay_keep, p_raw[h], 0.0)
            onward(h).start()

    def inner(h):
        @pl.when(near_ok)
        def _():
            direct(h).wait_recv()

        from_near = jnp.where(near_ok, near_in[h], 0.0)
        p_sum[h] = p_raw[h] + jnp.where(p_keep, from_near, 0.0)
        across(h).start()

        @pl.when(far_from_ok & jnp.logical_not(near_turn(h)))
        def _():
            far(h).wait_recv()

        use_far = x_keep & far_from_ok & jnp.logical_not(near_turn(h))
        close = (from_near + jnp.where(use_far, far_in[h], 0.0)).astype(jnp.bfloat16)
        xa, xb, pa, pb = xa_h[h], xb_h[h], pa_h[h], pb_h[h]
        m = mask[...]
        w1 = (m * dot(xa, pa, 1, 1)).astype(jnp.bfloat16)
        w2 = (m * dot(xb, pb, 1, 1)).astype(jnp.bfloat16)
        spot = pl.ds(h, rows, stride=heads)
        scale = x_scale[...]
        o1[spot, :] = dot(w1, pb, 1, 0) + scale * dot(xa, close, 1, 0)
        o2[spot, :] = dot(w2, pa, 1, 0) + scale * dot(xb, close, 1, 1)
        o3[spot, :] = dot(w2, xa, 0, 0)
        o4[spot, :] = dot(w1, xb, 0, 0)

    def outer(h):
        across(h).wait_recv()
        other = pair_in[h].astype(jnp.bfloat16)
        pa, pb = pa_h[h], pb_h[h]
        spot = pl.ds(h, rows, stride=heads)
        scale = p_scale[...]
        o3[spot, :] = o3[spot, :] + scale * dot(pb, other, 1, 1)
        o4[spot, :] = o4[spot, :] + scale * dot(pa, other, 1, 0)

    inner_lag, outer_lag = INNER_LAG, OUTER_LAG

    def turn(i, _):
        @pl.when(i < heads)
        def _():
            p_state(i)
            relay(i)

        @pl.when((i >= inner_lag) & (i < heads + inner_lag))
        def _():
            inner(i - inner_lag)

        @pl.when(i >= outer_lag)
        def _():
            outer(i - outer_lag)

        return 0

    lax.fori_loop(0, heads + outer_lag, turn, 0)

    remote(p_sum, pair_in, pair_send, pair_recv.at[0], pair).wait_send()

    @pl.when(near_ok)
    def _():
        remote(x_out, near_in, near_send, near_recv.at[0], near).wait_send()

    @pl.when(far_to_ok)
    def _():
        remote(p_raw, far_in, far_send, far_recv.at[0], far_to).wait_send()


def settle(i1, i2, i3, i4, att, gq, gk, gv, s1, s2, s3, s4, sem):
    rows, heads, width = s1.shape
    parts = sem.shape[1]
    span = rows // parts
    step = 16
    odd = lax.rem(lax.axis_index("seq"), 2) == 1
    stages = (s1, s2, s3, s4)
    forward, reverse = (att, gq, gk, gv), (gv, gk, gq, att)

    def put(i, part, dst):
        cut = pl.ds(part * span, span)
        return pltpu.make_async_copy(stages[i].at[cut], dst.at[cut], sem.at[i, part])

    for part in range(parts):
        def narrow(i, _):
            at = pl.multiple_of(part * span + i * step, step)
            for src, dst in zip((i1, i2, i3, i4), stages):
                block = src[pl.ds(at * heads, step * heads), :].reshape(step, heads, width)
                dst[pl.ds(at, step)] = block.astype(jnp.bfloat16)
            return 0

        lax.fori_loop(0, span // step, narrow, 0)

        @pl.when(odd)
        def _():
            for i in range(4):
                put(i, part, reverse[i]).start()

        @pl.when(jnp.logical_not(odd))
        def _():
            for i in range(4):
                put(i, part, forward[i]).start()

    for part in range(parts):
        for i in range(4):
            put(i, part, att).wait()


def local_paired(seq, queries, keys, values, cotangent, doc_lengths):
    rows, heads, width = queries.shape
    vmem = pl.BlockSpec(memory_space=pltpu.VMEM)
    hbm = pl.BlockSpec(memory_space=pltpu.HBM)
    whole = pltpu.VMEM((rows, heads, width), jnp.bfloat16)
    by_head = pltpu.VMEM((heads, rows, width), jnp.bfloat16)
    square = pltpu.VMEM((heads, width, width), jnp.float32)
    flat = jax.ShapeDtypeStruct((rows * heads, width), jnp.float32)
    each = pltpu.SemaphoreType.DMA((heads,))
    held = pl.pallas_call(
        functools.partial(paired, seq),
        out_shape=[flat] * 4,
        in_specs=[hbm] * 5,
        out_specs=[vmem] * 4,
        scratch_shapes=[pltpu.SMEM(doc_lengths.shape, jnp.int32)]
        + [whole] * 4
        + [by_head] * 4
        + [pltpu.VMEM((rows, rows), jnp.float32)]
        + [pltpu.VMEM((rows, width), jnp.bfloat16)] * 2
        + [pltpu.VMEM((rows, width), jnp.float32)] * 2
        + [square] * 8
        + [pltpu.SemaphoreType.DMA, pltpu.SemaphoreType.DMA((4, LOAD_PARTS))]
        + [pltpu.SemaphoreType.DMA] * 3
        + [each] * 4,
        compiler_params=pltpu.CompilerParams(
            collective_id=0, has_side_effects=True, vmem_limit_bytes=40 * 2**20
        ),
    )(*(pltpu.with_memory_space_constraint(a, pltpu.HBM) for a in (doc_lengths, queries, keys, values, cotangent)))
    return pl.pallas_call(
        settle,
        out_shape=[jax.ShapeDtypeStruct(queries.shape, jnp.bfloat16)] * 4,
        in_specs=[vmem] * 4,
        out_specs=[hbm] * 4,
        scratch_shapes=[whole] * 4 + [pltpu.SemaphoreType.DMA((4, STORE_PARTS))],
        compiler_params=pltpu.CompilerParams(vmem_limit_bytes=24 * 2**20),
    )(*held)


def local(seq, queries, keys, values, cotangent, doc_lengths):
    rows, heads, width = queries.shape
    longest = seq * rows // LONGEST_PART
    hops = min(seq - 1, (longest - 1 + rows - 1) // rows)
    if hops == 2 and seq % 2 == 0:
        return local_paired(seq, queries, keys, values, cotangent, doc_lengths)
    vmem = pl.BlockSpec(memory_space=pltpu.VMEM)
    flat = pltpu.VMEM((rows * heads, width), jnp.float32)
    by_head = pltpu.VMEM((heads, rows, width), jnp.bfloat16)
    whole = pltpu.VMEM((rows, heads, width), jnp.bfloat16)
    square = pltpu.VMEM((heads, width, width), jnp.float32)
    squares = pltpu.VMEM((hops, heads, width, width), jnp.float32)
    return pl.pallas_call(
        functools.partial(kernel, seq, hops),
        out_shape=[jax.ShapeDtypeStruct(queries.shape, jnp.bfloat16)] * 4,
        in_specs=[pl.BlockSpec(memory_space=pltpu.SMEM)]
        + [pl.BlockSpec(memory_space=pltpu.HBM)] * 4,
        out_specs=[vmem] * 4,
        scratch_shapes=[whole] * 4
        + [flat] * 4
        + [by_head] * 4
        + [pltpu.VMEM((rows, rows), jnp.float32), square, square, squares, squares,
           pltpu.VMEM((2, heads, width, width), jnp.float32)]
        + [pltpu.SemaphoreType.DMA((4,)), pltpu.SemaphoreType.DMA((2, heads)), pltpu.SemaphoreType.DMA((2, heads))]
        + [pltpu.SemaphoreType.DMA((hops, heads))] * 4,
        compiler_params=pltpu.CompilerParams(
            collective_id=0, has_side_effects=True, vmem_limit_bytes=49 * 2**20
        ),
    )(doc_lengths, queries, keys, values, cotangent)


def solution(mesh):
    spec = P(("dp", "seq"), None, None)
    return jax.shard_map(
        functools.partial(local, mesh.shape["seq"]),
        mesh=mesh,
        in_specs=(spec, spec, spec, spec, P("dp")),
        out_specs=(spec, spec, spec, spec),
        check_vma=False,
    )
```

```python
import functools

import jax
import jax.numpy as jnp
from jax import lax
from jax.experimental import pallas as pl
from jax.experimental.pallas import tpu as pltpu
from jax.sharding import PartitionSpec as P

BLOCK = 256
LONGEST_PART = 4
MESH = pl.DeviceIdType.MESH
INNER_LAG, OUTER_LAG = 6, 9
LOAD_PARTS, STORE_PARTS = 2, 4


def dot(a, b, ca, cb):
    return lax.dot_general(
        a, b, (((ca,), (cb,)), ((), ())), preferred_element_type=jnp.float32
    )


def kernel(
    seq, hops,
    lengths, q_hbm, k_hbm, v_hbm, c_hbm,
    att_out, gq_out, gk_out, gv_out,
    q_in, k_in, v_in, c_in, qf, kf, vf, cf, qh, kh, vh, ch,
    mask, state, ret, state_in, ret_in, relay_in,
    load_sem, relay_send, relay_recv, state_send, state_recv, ret_send, ret_recv,
):
    rows, heads, width = q_in.shape
    loads = [
        pltpu.make_async_copy(src, dst, load_sem.at[i])
        for i, (src, dst) in enumerate(
            ((k_hbm, k_in), (v_hbm, v_in), (q_hbm, q_in), (c_hbm, c_in))
        )
    ]
    for load in loads:
        load.start()
    factor = (width * BLOCK) ** (-0.5)
    dp, me = lax.axis_index("dp"), lax.axis_index("seq")
    first = me * rows
    last = first + rows - 1

    barrier = pltpu.get_barrier_semaphore()
    for d in range(1, hops + 1):
        for ok, peer in ((me + d < seq, me + d), (me - d >= 0, me - d)):
            @pl.when(ok)
            def _(peer=peer):
                pl.semaphore_signal(barrier, inc=1, device_id=(dp, peer), device_id_type=MESH)

    for d in range(hops):
        @pl.when(me - d - 1 < 0)
        def _(d=d):
            state_in[d] = jnp.zeros(state_in.shape[1:], state_in.dtype)

        @pl.when(me + d + 1 >= seq)
        def _(d=d):
            ret_in[d] = jnp.zeros(ret_in.shape[1:], ret_in.dtype)

    big = jnp.int32(2**30)
    zero = jnp.int32(0)
    ends = []
    total = zero
    for j in range(lengths.shape[0]):
        total = total + lengths[j]
        ends.append(total)

    def start_of(p):
        out = zero
        for e in ends:
            out = jnp.maximum(out, jnp.where(e <= p, e, zero))
        return out

    def end_of(p):
        out = big
        for e in ends:
            out = jnp.minimum(out, jnp.where(e > p, e, big))
        return out

    tail_start = start_of(last + 1)
    head_end_prev = end_of(first - 1)
    head_start, head_end = start_of(first), end_of(first)
    last_start, last_end = start_of(last), end_of(last)

    step = 16

    def widen(*pairs):
        def part(i, _):
            at = pl.multiple_of(i * step, step)
            for src, dst in pairs:
                block = src[pl.ds(at, step)].astype(jnp.float32)
                dst[pl.ds(at * heads, step * heads), :] = block.reshape(step * heads, width)
            return 0

        lax.fori_loop(0, rows // step, part, 0)

    pl.semaphore_wait(barrier, jnp.minimum(me, hops) + jnp.minimum(seq - 1 - me, hops))

    pos = first + lax.broadcasted_iota(jnp.int32, (rows, width), 0)
    in_tail = pos >= tail_start
    in_head = pos < head_end_prev

    def forward(d, h):
        return pltpu.make_async_remote_copy(
            src_ref=state.at[h], dst_ref=state_in.at[d, h],
            send_sem=state_send.at[d, h], recv_sem=state_recv.at[d, h],
            device_id=(dp, me + d + 1), device_id_type=MESH,
        )

    def backward(d, h):
        return pltpu.make_async_remote_copy(
            src_ref=ret.at[h], dst_ref=ret_in.at[d, h],
            send_sem=ret_send.at[d, h], recv_sem=ret_recv.at[d, h],
            device_id=(dp, me - d - 1), device_id_type=MESH,
        )

    levels = max(seq // 2, 1)
    odd = lax.rem(me, 2) == 1
    even = lax.rem(me, 2) == 0
    level = me // 2
    up, down = me + 1 < seq, me >= 1

    def state_turn(h):
        return lax.rem(h, levels) < levels - 1 - level

    def ret_turn(h):
        return lax.rem(h, levels) < level

    def state_via(h):
        return odd & up & state_turn(h)

    def state_relays(h):
        return even & (me + 2 < seq) & state_turn(h)

    def ret_via(h):
        return even & (me >= 2) & up & ret_turn(h)

    def ret_relays(h):
        return odd & (me >= 2) & ret_turn(h)

    def via_state(h):
        return pltpu.make_async_remote_copy(
            src_ref=state.at[h], dst_ref=relay_in.at[0, h],
            send_sem=state_send.at[0, h], recv_sem=relay_recv.at[0, h],
            device_id=(dp, me - 1), device_id_type=MESH,
        )

    def via_ret(h):
        return pltpu.make_async_remote_copy(
            src_ref=ret.at[h], dst_ref=relay_in.at[1, h],
            send_sem=ret_send.at[0, h], recv_sem=relay_recv.at[1, h],
            device_id=(dp, me + 1), device_id_type=MESH,
        )

    def relay_state(h):
        return pltpu.make_async_remote_copy(
            src_ref=relay_in.at[0, h], dst_ref=state_in.at[0, h],
            send_sem=relay_send.at[0, h], recv_sem=state_recv.at[0, h],
            device_id=(dp, me + 2), device_id_type=MESH,
        )

    def relay_ret(h):
        return pltpu.make_async_remote_copy(
            src_ref=relay_in.at[1, h], dst_ref=ret_in.at[0, h],
            send_sem=relay_send.at[1, h], recv_sem=ret_recv.at[0, h],
            device_id=(dp, me - 2), device_id_type=MESH,
        )

    def sends_state(d, h):
        if d == 0 and hops > 1:
            return up & jnp.logical_not(state_via(h))
        return me + d + 1 < seq

    def sends_ret(d, h):
        if d == 0 and hops > 1:
            return down & jnp.logical_not(ret_via(h))
        return me - d - 1 >= 0

    def arrived_state(h):
        return pltpu.make_async_remote_copy(
            src_ref=state.at[h], dst_ref=relay_in.at[0, h],
            send_sem=state_send.at[0, h], recv_sem=relay_recv.at[0, h],
            device_id=(dp, me + 1), device_id_type=MESH,
        )

    def arrived_ret(h):
        return pltpu.make_async_remote_copy(
            src_ref=ret.at[h], dst_ref=relay_in.at[1, h],
            send_sem=ret_send.at[0, h], recv_sem=relay_recv.at[1, h],
            device_id=(dp, me - 1), device_id_type=MESH,
        )

    def relay(h):
        if hops > 1:
            @pl.when(state_relays(h))
            def _():
                arrived_state(h).wait_recv()
                relay_state(h).start()

            @pl.when(ret_relays(h))
            def _():
                arrived_ret(h).wait_recv()
                relay_ret(h).start()

    def state_sum(h):
        k32 = kf[pl.ds(h, rows, stride=heads), :]
        v16 = vf[pl.ds(h, rows, stride=heads), :].astype(jnp.bfloat16)
        kh[h] = k32.astype(jnp.bfloat16)
        vh[h] = v16
        state[h] = dot(jnp.where(in_tail, k32, 0.0).astype(jnp.bfloat16), v16, 0, 0)
        if hops > 1:
            @pl.when(state_via(h))
            def _():
                via_state(h).start()

        for d in range(hops):
            @pl.when(sends_state(d, h))
            def _(d=d):
                forward(d, h).start()

    def ret_sum(h):
        q32 = qf[pl.ds(h, rows, stride=heads), :]
        c16 = cf[pl.ds(h, rows, stride=heads), :].astype(jnp.bfloat16)
        qh[h] = q32.astype(jnp.bfloat16)
        ch[h] = c16
        ret[h] = dot(jnp.where(in_head, q32, 0.0).astype(jnp.bfloat16), c16, 0, 0)
        if hops > 1:
            @pl.when(ret_via(h))
            def _():
                via_ret(h).start()

        for d in range(hops):
            @pl.when(sends_ret(d, h))
            def _(d=d):
                backward(d, h).start()

    def each(fn):
        def body(h, _):
            fn(h)
            return 0

        return body

    ahead = min(4, heads)
    loads[0].wait()
    loads[1].wait()
    widen((k_in, kf), (v_in, vf))
    lax.fori_loop(0, ahead, each(state_sum), 0)
    loads[2].wait()
    loads[3].wait()
    widen((q_in, qf), (c_in, cf))

    def both(h):
        ret_sum(h)
        state_sum(h + ahead)

    lax.fori_loop(0, heads - ahead, each(both), 0)
    lax.fori_loop(heads - ahead, heads, each(ret_sum), 0)

    t_pos = first + lax.broadcasted_iota(jnp.int32, (rows, rows), 0)
    s_pos = first + lax.broadcasted_iota(jnp.int32, (rows, rows), 1)
    col = first + lax.broadcasted_iota(jnp.int32, (rows, 1), 0)
    begin = jnp.zeros((rows, 1), jnp.int32)
    for e in ends:
        begin = jnp.maximum(begin, jnp.where(col >= e, e, 0))
    visible = (s_pos <= t_pos) & (s_pos >= begin)
    mask[...] = jnp.where(visible, factor, 0.0).astype(jnp.float32)

    lead = heads // 8

    def inside(h, _):
        @pl.when(h >= heads // 2 - lead)
        def _():
            relay(h - (heads // 2 - lead))

        q, k, v, c = qh[h], kh[h], vh[h], ch[h]
        m = mask[...]
        weights = (m * dot(q, k, 1, 1)).astype(jnp.bfloat16)
        grad_weights = (m * dot(c, v, 1, 1)).astype(jnp.bfloat16)
        spot = pl.ds(h, rows, stride=heads)
        qf[spot, :] = dot(weights, v, 1, 0)
        kf[spot, :] = dot(grad_weights, k, 1, 0)
        vf[spot, :] = dot(grad_weights, q, 0, 0)
        cf[spot, :] = dot(weights, c, 0, 0)
        return 0

    lax.fori_loop(0, heads, inside, 0)

    head_factor = jnp.where(pos < head_end, factor, 0.0).astype(jnp.float32)
    tail_factor = jnp.where(pos >= last_start, factor, 0.0).astype(jnp.float32)

    def outside(h, _):
        carried = jnp.zeros((width, width), jnp.float32)
        returned = jnp.zeros((width, width), jnp.float32)
        @pl.when((h >= heads - heads // 2) & (h + lead < heads))
        def _():
            relay(h + lead)

        for d in range(hops):
            @pl.when(me - d - 1 >= 0)
            def _(d=d):
                forward(d, h).wait_recv()

            @pl.when(me + d + 1 < seq)
            def _(d=d):
                backward(d, h).wait_recv()

            here = head_start <= first - d * rows
            carried = carried + jnp.where(here, state_in[d, h], 0.0)
            there = last_end >= last + d * rows + 1
            returned = returned + jnp.where(there, ret_in[d, h], 0.0)
        carried = carried.astype(jnp.bfloat16)
        returned = returned.astype(jnp.bfloat16)
        q, k, v, c = qh[h], kh[h], vh[h], ch[h]
        spot = pl.ds(h, rows, stride=heads)
        qf[spot, :] = qf[spot, :] + head_factor * dot(q, carried, 1, 0)
        kf[spot, :] = kf[spot, :] + head_factor * dot(c, carried, 1, 1)
        vf[spot, :] = vf[spot, :] + tail_factor * dot(v, returned, 1, 1)
        cf[spot, :] = cf[spot, :] + tail_factor * dot(k, returned, 1, 0)
        return 0

    lax.fori_loop(0, heads, outside, 0)

    def narrow(i, _):
        at = pl.multiple_of(i * step, step)
        for src, dst in ((qf, att_out), (kf, gq_out), (vf, gk_out), (cf, gv_out)):
            block = src[pl.ds(at * heads, step * heads), :].reshape(step, heads, width)
            dst[pl.ds(at, step)] = block.astype(jnp.bfloat16)
        return 0

    lax.fori_loop(0, rows // step, narrow, 0)

    def drain(h):
        for d in range(hops):
            @pl.when(sends_state(d, h))
            def _(d=d):
                forward(d, h).wait_send()

            @pl.when(sends_ret(d, h))
            def _(d=d):
                backward(d, h).wait_send()

        if hops > 1:
            @pl.when(state_via(h))
            def _():
                via_state(h).wait_send()

            @pl.when(ret_via(h))
            def _():
                via_ret(h).wait_send()

            @pl.when(state_relays(h))
            def _():
                relay_state(h).wait_send()

            @pl.when(ret_relays(h))
            def _():
                relay_ret(h).wait_send()

    lax.fori_loop(0, heads, each(drain), 0)


def paired(
    seq,
    lens_hbm, q_hbm, k_hbm, v_hbm, c_hbm,
    o1, o2, o3, o4,
    lengths, xa_in, xb_in, pa_in, pb_in, xa_h, xb_h, pa_h, pb_h,
    mask, x_rows, p_rows, x_scale, p_scale,
    x_out, p_raw, p_sum, near_in, far_in, pair_in, relay_in, relay_sum,
    len_sem, load_sem, near_send, far_send, pair_send,
    near_recv, side_recv, pair_recv,
):
    rows, heads, width = xa_in.shape
    factor = (width * BLOCK) ** (-0.5)
    dp, me = lax.axis_index("dp"), lax.axis_index("seq")
    odd = lax.rem(me, 2) == 1
    even = jnp.logical_not(odd)
    toward = jnp.where(odd, 1, -1)
    first = me * rows
    last = first + rows - 1
    near, pair = me + toward, me - toward
    far_to, far_from = me - 2 * toward, me + 2 * toward
    near_ok = (near >= 0) & (near < seq)
    far_to_ok = (far_to >= 0) & (far_to < seq)
    far_from_ok = (far_from >= 0) & (far_from < seq)

    barrier = pltpu.get_barrier_semaphore()
    for ok, peer in ((near_ok, near), (pair >= 0, pair), (far_to_ok, far_to), (far_from_ok, far_from)):
        @pl.when(ok)
        def _(peer=peer):
            pl.semaphore_signal(barrier, inc=1, device_id=(dp, peer), device_id_type=MESH)

    parts = load_sem.shape[1]
    span = rows // parts

    len_load = pltpu.make_async_copy(lens_hbm, lengths, len_sem)
    len_load.start()

    def load(i, part, src, dst):
        cut = pl.ds(part * span, span)
        return pltpu.make_async_copy(src.at[cut], dst.at[cut], load_sem.at[i, part])

    landing = (xa_in, xb_in, pa_in, pb_in)

    @pl.when(even)
    def _():
        for pair in (0, 2):
            for part in range(parts):
                for i in (pair, pair + 1):
                    load(i, part, (q_hbm, c_hbm, k_hbm, v_hbm)[i], landing[i]).start()

    @pl.when(odd)
    def _():
        for pair in (0, 2):
            for part in range(parts):
                for i in (pair, pair + 1):
                    load(i, part, (k_hbm, v_hbm, q_hbm, c_hbm)[i], landing[i]).start()

    len_load.wait()
    big = jnp.int32(2**30)
    zero = jnp.int32(0)
    ends = []
    total = zero
    for j in range(lengths.shape[0]):
        total = total + lengths[j]
        ends.append(total)

    def start_of(p):
        out = zero
        for e in ends:
            out = jnp.maximum(out, jnp.where(e <= p, e, zero))
        return out

    def end_of(p):
        out = big
        for e in ends:
            out = jnp.minimum(out, jnp.where(e > p, e, big))
        return out

    tail_start = start_of(last + 1)
    head_end_prev = end_of(first - 1)
    head_start, head_end = start_of(first), end_of(first)
    last_start, last_end = start_of(last), end_of(last)
    x_keep = jnp.where(odd, last_end >= last + rows + 1, head_start <= first - rows)
    p_keep = jnp.where(odd, head_end_prev >= last + 1, tail_start <= first)
    relay_keep = jnp.where(odd, end_of(first - rows - 1) >= first, start_of(last + rows + 1) <= last + 1)

    pos = first + lax.broadcasted_iota(jnp.int32, (rows, width), 0)
    x_low, x_high = jnp.where(odd, tail_start, zero), jnp.where(odd, big, head_end_prev)
    p_low, p_high = jnp.where(odd, zero, tail_start), jnp.where(odd, head_end_prev, big)
    x_rows[...] = jnp.where((pos >= x_low) & (pos < x_high), 1.0, 0.0).astype(jnp.bfloat16)

    step = 16

    def widen(part, *pairs):
        def some(i, _):
            at = pl.multiple_of(part * span + i * step, step)
            for src, dst in pairs:
                block = src[pl.ds(at, step)].astype(jnp.float32)
                dst[pl.ds(at * heads, step * heads), :] = block.reshape(step * heads, width)
            return 0

        lax.fori_loop(0, span // step, some, 0)

    levels = seq // 2
    level = me // 2
    mine = jnp.where(odd, levels - 1 - level, level)
    theirs = levels - 1 - mine

    eased = (dp == 0) & even

    def my_turn(h):
        kept = (dp > 0) | even | (level > 0) | (h != heads - 2)
        return (lax.rem(h, levels) < mine) & kept

    def their_turn(h):
        kept = jnp.logical_not(eased & (level == 0) & (h == heads - 2))
        return (lax.rem(h, levels) < theirs) & kept

    def near_turn(h):
        kept = jnp.logical_not(eased & (level == 1) & (h == heads - 2))
        return (lax.rem(h, levels) < jnp.where(odd, level + 1, levels - level)) & kept

    def remote(src, dst, send, recv, peer):
        return pltpu.make_async_remote_copy(
            src_ref=src, dst_ref=dst, send_sem=send, recv_sem=recv,
            device_id=(dp, peer), device_id_type=MESH,
        )

    def direct(h):
        return remote(x_out.at[h], near_in.at[h], near_send, near_recv.at[h], near)

    def via(h):
        return remote(x_out.at[h], relay_in.at[h], near_send, side_recv.at[h], pair)

    def onward(h):
        return remote(relay_sum.at[h], near_in.at[h], far_send, near_recv.at[h], far_to)

    def far(h):
        return remote(p_raw.at[h], far_in.at[h], far_send, side_recv.at[h], far_to)

    def across(h):
        return remote(p_sum.at[h], pair_in.at[h], pair_send, pair_recv.at[h], pair)

    for part in range(parts):
        for i in (0, 1):
            load(i, part, q_hbm, landing[i]).wait()
        widen(part, (xa_in, o1), (xb_in, o2))

    pl.semaphore_wait(
        barrier, 1 + near_ok.astype(jnp.int32) + far_to_ok.astype(jnp.int32) + far_from_ok.astype(jnp.int32)
    )

    def x_state(h, _):
        spot = pl.ds(h, rows, stride=heads)
        xa = o1[spot, :].astype(jnp.bfloat16)
        xb = o2[spot, :].astype(jnp.bfloat16)
        xa_h[h] = xa
        xb_h[h] = xb

        @pl.when(near_ok)
        def _():
            x_out[h] = dot(xa * x_rows[...], xb, 0, 0)

        @pl.when(my_turn(h))
        def _():
            via(h).start()

        @pl.when(near_ok & jnp.logical_not(my_turn(h)))
        def _():
            direct(h).start()

        return 0

    lax.fori_loop(0, heads, x_state, 0)

    p_rows[...] = jnp.where((pos >= p_low) & (pos < p_high), 1.0, 0.0).astype(jnp.bfloat16)
    in_head, in_tail = pos < head_end, pos >= last_start
    head_scale = jnp.where(in_head, factor, 0.0).astype(jnp.float32)
    tail_scale = jnp.where(in_tail, factor, 0.0).astype(jnp.float32)
    x_scale[...] = jnp.where(odd, tail_scale, head_scale)
    p_scale[...] = jnp.where(odd, head_scale, tail_scale)
    col = first + lax.broadcasted_iota(jnp.int32, (1, rows), 1)
    begin = jnp.zeros((1, rows), jnp.int32)
    finish = jnp.full((1, rows), big, jnp.int32)
    for e in ends:
        begin = jnp.maximum(begin, jnp.where(col >= e, e, zero))
        finish = jnp.minimum(finish, jnp.where(col < e, e, big))
    low, high = jnp.where(odd, begin, col), jnp.where(odd, col + 1, finish)
    row = first + lax.broadcasted_iota(jnp.int32, (rows, rows), 0)
    mask[...] = jnp.where((row >= low) & (row < high), factor, 0.0).astype(jnp.float32)

    for part in range(parts):
        for i in (2, 3):
            load(i, part, q_hbm, landing[i]).wait()
        widen(part, (pa_in, o3), (pb_in, o4))

    def p_state(h):
        spot = pl.ds(h, rows, stride=heads)
        pa = o3[spot, :].astype(jnp.bfloat16)
        pb = o4[spot, :].astype(jnp.bfloat16)
        pa_h[h] = pa
        pb_h[h] = pb
        p_raw[h] = dot(pa * p_rows[...], pb, 0, 0)

        @pl.when(far_to_ok & jnp.logical_not(their_turn(h)))
        def _():
            far(h).start()

    def relay(h):
        @pl.when(their_turn(h))
        def _():
            remote(x_out.at[h], relay_in.at[h], near_send, side_recv.at[h], pair).wait_recv()
            relay_sum[h] = relay_in[h] + jnp.where(relay_keep, p_raw[h], 0.0)
            onward(h).start()

    def inner(h):
        @pl.when(near_ok)
        def _():
            direct(h).wait_recv()

        from_near = jnp.where(near_ok, near_in[h], 0.0)
        p_sum[h] = p_raw[h] + jnp.where(p_keep, from_near, 0.0)
        across(h).start()

        @pl.when(far_from_ok & jnp.logical_not(near_turn(h)))
        def _():
            far(h).wait_recv()

        use_far = x_keep & far_from_ok & jnp.logical_not(near_turn(h))
        close = (from_near + jnp.where(use_far, far_in[h], 0.0)).astype(jnp.bfloat16)
        xa, xb, pa, pb = xa_h[h], xb_h[h], pa_h[h], pb_h[h]
        m = mask[...]
        w1 = (m * dot(xa, pa, 1, 1)).astype(jnp.bfloat16)
        w2 = (m * dot(xb, pb, 1, 1)).astype(jnp.bfloat16)
        spot = pl.ds(h, rows, stride=heads)
        scale = x_scale[...]
        o1[spot, :] = dot(w1, pb, 1, 0) + scale * dot(xa, close, 1, 0)
        o2[spot, :] = dot(w2, pa, 1, 0) + scale * dot(xb, close, 1, 1)
        o3[spot, :] = dot(w2, xa, 0, 0)
        o4[spot, :] = dot(w1, xb, 0, 0)

    def outer(h):
        across(h).wait_recv()
        other = pair_in[h].astype(jnp.bfloat16)
        pa, pb = pa_h[h], pb_h[h]
        spot = pl.ds(h, rows, stride=heads)
        scale = p_scale[...]
        o3[spot, :] = o3[spot, :] + scale * dot(pb, other, 1, 1)
        o4[spot, :] = o4[spot, :] + scale * dot(pa, other, 1, 0)

    inner_lag, outer_lag = INNER_LAG, OUTER_LAG

    def turn(i, _):
        @pl.when(i < heads)
        def _():
            p_state(i)
            relay(i)

        @pl.when((i >= inner_lag) & (i < heads + inner_lag))
        def _():
            inner(i - inner_lag)

        @pl.when(i >= outer_lag)
        def _():
            outer(i - outer_lag)

        return 0

    lax.fori_loop(0, heads + outer_lag, turn, 0)

    remote(p_sum, pair_in, pair_send, pair_recv.at[0], pair).wait_send()

    @pl.when(near_ok)
    def _():
        remote(x_out, near_in, near_send, near_recv.at[0], near).wait_send()

    @pl.when(far_to_ok)
    def _():
        remote(p_raw, far_in, far_send, side_recv.at[0], far_to).wait_send()


def settle(i1, i2, i3, i4, att, gq, gk, gv, s1, s2, s3, s4, sem):
    rows, heads, width = s1.shape
    parts = sem.shape[1]
    span = rows // parts
    step = 16
    odd = lax.rem(lax.axis_index("seq"), 2) == 1
    stages = (s1, s2, s3, s4)
    forward, reverse = (att, gq, gk, gv), (gv, gk, gq, att)

    def put(i, part, dst):
        cut = pl.ds(part * span, span)
        return pltpu.make_async_copy(stages[i].at[cut], dst.at[cut], sem.at[i, part])

    for part in range(parts):
        def narrow(i, _):
            at = pl.multiple_of(part * span + i * step, step)
            for src, dst in zip((i1, i2, i3, i4), stages):
                block = src[pl.ds(at * heads, step * heads), :].reshape(step, heads, width)
                dst[pl.ds(at, step)] = block.astype(jnp.bfloat16)
            return 0

        lax.fori_loop(0, span // step, narrow, 0)

        @pl.when(odd)
        def _():
            for i in range(4):
                put(i, part, reverse[i]).start()

        @pl.when(jnp.logical_not(odd))
        def _():
            for i in range(4):
                put(i, part, forward[i]).start()

    for part in range(parts):
        for i in range(4):
            put(i, part, att).wait()


def local_paired(seq, queries, keys, values, cotangent, doc_lengths):
    rows, heads, width = queries.shape
    vmem = pl.BlockSpec(memory_space=pltpu.VMEM)
    hbm = pl.BlockSpec(memory_space=pltpu.HBM)
    whole = pltpu.VMEM((rows, heads, width), jnp.bfloat16)
    by_head = pltpu.VMEM((heads, rows, width), jnp.bfloat16)
    square = pltpu.VMEM((heads, width, width), jnp.float32)
    flat = jax.ShapeDtypeStruct((rows * heads, width), jnp.float32)
    each = pltpu.SemaphoreType.DMA((heads,))
    held = pl.pallas_call(
        functools.partial(paired, seq),
        out_shape=[flat] * 4,
        in_specs=[hbm] * 5,
        out_specs=[vmem] * 4,
        scratch_shapes=[pltpu.SMEM(doc_lengths.shape, jnp.int32)]
        + [whole] * 4
        + [by_head] * 4
        + [pltpu.VMEM((rows, rows), jnp.float32)]
        + [pltpu.VMEM((rows, width), jnp.bfloat16)] * 2
        + [pltpu.VMEM((rows, width), jnp.float32)] * 2
        + [square] * 8
        + [pltpu.SemaphoreType.DMA, pltpu.SemaphoreType.DMA((4, LOAD_PARTS))]
        + [pltpu.SemaphoreType.DMA] * 3
        + [each] * 3,
        compiler_params=pltpu.CompilerParams(
            collective_id=0, has_side_effects=True, vmem_limit_bytes=40 * 2**20
        ),
    )(*(pltpu.with_memory_space_constraint(a, pltpu.HBM) for a in (doc_lengths, queries, keys, values, cotangent)))
    return pl.pallas_call(
        settle,
        out_shape=[jax.ShapeDtypeStruct(queries.shape, jnp.bfloat16)] * 4,
        in_specs=[vmem] * 4,
        out_specs=[hbm] * 4,
        scratch_shapes=[whole] * 4 + [pltpu.SemaphoreType.DMA((4, STORE_PARTS))],
        compiler_params=pltpu.CompilerParams(vmem_limit_bytes=24 * 2**20),
    )(*held)


def local(seq, queries, keys, values, cotangent, doc_lengths):
    rows, heads, width = queries.shape
    longest = seq * rows // LONGEST_PART
    hops = min(seq - 1, (longest - 1 + rows - 1) // rows)
    if hops == 2 and seq % 2 == 0:
        return local_paired(seq, queries, keys, values, cotangent, doc_lengths)
    vmem = pl.BlockSpec(memory_space=pltpu.VMEM)
    flat = pltpu.VMEM((rows * heads, width), jnp.float32)
    by_head = pltpu.VMEM((heads, rows, width), jnp.bfloat16)
    whole = pltpu.VMEM((rows, heads, width), jnp.bfloat16)
    square = pltpu.VMEM((heads, width, width), jnp.float32)
    squares = pltpu.VMEM((hops, heads, width, width), jnp.float32)
    return pl.pallas_call(
        functools.partial(kernel, seq, hops),
        out_shape=[jax.ShapeDtypeStruct(queries.shape, jnp.bfloat16)] * 4,
        in_specs=[pl.BlockSpec(memory_space=pltpu.SMEM)]
        + [pl.BlockSpec(memory_space=pltpu.HBM)] * 4,
        out_specs=[vmem] * 4,
        scratch_shapes=[whole] * 4
        + [flat] * 4
        + [by_head] * 4
        + [pltpu.VMEM((rows, rows), jnp.float32), square, square, squares, squares,
           pltpu.VMEM((2, heads, width, width), jnp.float32)]
        + [pltpu.SemaphoreType.DMA((4,)), pltpu.SemaphoreType.DMA((2, heads)), pltpu.SemaphoreType.DMA((2, heads))]
        + [pltpu.SemaphoreType.DMA((hops, heads))] * 4,
        compiler_params=pltpu.CompilerParams(
            collective_id=0, has_side_effects=True, vmem_limit_bytes=49 * 2**20
        ),
    )(doc_lengths, queries, keys, values, cotangent)


def solution(mesh):
    spec = P(("dp", "seq"), None, None)
    return jax.shard_map(
        functools.partial(local, mesh.shape["seq"]),
        mesh=mesh,
        in_specs=(spec, spec, spec, spec, P("dp")),
        out_specs=(spec, spec, spec, spec),
        check_vma=False,
    )
```

```python
import functools

import jax
import jax.numpy as jnp
from jax import lax
from jax.experimental import pallas as pl
from jax.experimental.pallas import tpu as pltpu
from jax.sharding import PartitionSpec as P

BLOCK = 256
LONGEST_PART = 4
MESH = pl.DeviceIdType.MESH
INNER_LAG, OUTER_LAG = 6, 9
LOAD_PARTS, STORE_PARTS = 2, 4


def dot(a, b, ca, cb):
    return lax.dot_general(
        a, b, (((ca,), (cb,)), ((), ())), preferred_element_type=jnp.float32
    )


def kernel(
    seq, hops,
    lengths, q_hbm, k_hbm, v_hbm, c_hbm,
    att_out, gq_out, gk_out, gv_out,
    q_in, k_in, v_in, c_in, qf, kf, vf, cf, qh, kh, vh, ch,
    mask, state, ret, state_in, ret_in, relay_in,
    load_sem, relay_send, relay_recv, state_send, state_recv, ret_send, ret_recv,
):
    rows, heads, width = q_in.shape
    loads = [
        pltpu.make_async_copy(src, dst, load_sem.at[i])
        for i, (src, dst) in enumerate(
            ((k_hbm, k_in), (v_hbm, v_in), (q_hbm, q_in), (c_hbm, c_in))
        )
    ]
    for load in loads:
        load.start()
    factor = (width * BLOCK) ** (-0.5)
    dp, me = lax.axis_index("dp"), lax.axis_index("seq")
    first = me * rows
    last = first + rows - 1

    barrier = pltpu.get_barrier_semaphore()
    for d in range(1, hops + 1):
        for ok, peer in ((me + d < seq, me + d), (me - d >= 0, me - d)):
            @pl.when(ok)
            def _(peer=peer):
                pl.semaphore_signal(barrier, inc=1, device_id=(dp, peer), device_id_type=MESH)

    for d in range(hops):
        @pl.when(me - d - 1 < 0)
        def _(d=d):
            state_in[d] = jnp.zeros(state_in.shape[1:], state_in.dtype)

        @pl.when(me + d + 1 >= seq)
        def _(d=d):
            ret_in[d] = jnp.zeros(ret_in.shape[1:], ret_in.dtype)

    big = jnp.int32(2**30)
    zero = jnp.int32(0)
    ends = []
    total = zero
    for j in range(lengths.shape[0]):
        total = total + lengths[j]
        ends.append(total)

    def start_of(p):
        out = zero
        for e in ends:
            out = jnp.maximum(out, jnp.where(e <= p, e, zero))
        return out

    def end_of(p):
        out = big
        for e in ends:
            out = jnp.minimum(out, jnp.where(e > p, e, big))
        return out

    tail_start = start_of(last + 1)
    head_end_prev = end_of(first - 1)
    head_start, head_end = start_of(first), end_of(first)
    last_start, last_end = start_of(last), end_of(last)

    step = 16

    def widen(*pairs):
        def part(i, _):
            at = pl.multiple_of(i * step, step)
            for src, dst in pairs:
                block = src[pl.ds(at, step)].astype(jnp.float32)
                dst[pl.ds(at * heads, step * heads), :] = block.reshape(step * heads, width)
            return 0

        lax.fori_loop(0, rows // step, part, 0)

    pl.semaphore_wait(barrier, jnp.minimum(me, hops) + jnp.minimum(seq - 1 - me, hops))

    pos = first + lax.broadcasted_iota(jnp.int32, (rows, width), 0)
    in_tail = pos >= tail_start
    in_head = pos < head_end_prev

    def forward(d, h):
        return pltpu.make_async_remote_copy(
            src_ref=state.at[h], dst_ref=state_in.at[d, h],
            send_sem=state_send.at[d, h], recv_sem=state_recv.at[d, h],
            device_id=(dp, me + d + 1), device_id_type=MESH,
        )

    def backward(d, h):
        return pltpu.make_async_remote_copy(
            src_ref=ret.at[h], dst_ref=ret_in.at[d, h],
            send_sem=ret_send.at[d, h], recv_sem=ret_recv.at[d, h],
            device_id=(dp, me - d - 1), device_id_type=MESH,
        )

    levels = max(seq // 2, 1)
    odd = lax.rem(me, 2) == 1
    even = lax.rem(me, 2) == 0
    level = me // 2
    up, down = me + 1 < seq, me >= 1

    def state_turn(h):
        return lax.rem(h, levels) < levels - 1 - level

    def ret_turn(h):
        return lax.rem(h, levels) < level

    def state_via(h):
        return odd & up & state_turn(h)

    def state_relays(h):
        return even & (me + 2 < seq) & state_turn(h)

    def ret_via(h):
        return even & (me >= 2) & up & ret_turn(h)

    def ret_relays(h):
        return odd & (me >= 2) & ret_turn(h)

    def via_state(h):
        return pltpu.make_async_remote_copy(
            src_ref=state.at[h], dst_ref=relay_in.at[0, h],
            send_sem=state_send.at[0, h], recv_sem=relay_recv.at[0, h],
            device_id=(dp, me - 1), device_id_type=MESH,
        )

    def via_ret(h):
        return pltpu.make_async_remote_copy(
            src_ref=ret.at[h], dst_ref=relay_in.at[1, h],
            send_sem=ret_send.at[0, h], recv_sem=relay_recv.at[1, h],
            device_id=(dp, me + 1), device_id_type=MESH,
        )

    def relay_state(h):
        return pltpu.make_async_remote_copy(
            src_ref=relay_in.at[0, h], dst_ref=state_in.at[0, h],
            send_sem=relay_send.at[0, h], recv_sem=state_recv.at[0, h],
            device_id=(dp, me + 2), device_id_type=MESH,
        )

    def relay_ret(h):
        return pltpu.make_async_remote_copy(
            src_ref=relay_in.at[1, h], dst_ref=ret_in.at[0, h],
            send_sem=relay_send.at[1, h], recv_sem=ret_recv.at[0, h],
            device_id=(dp, me - 2), device_id_type=MESH,
        )

    def sends_state(d, h):
        if d == 0 and hops > 1:
            return up & jnp.logical_not(state_via(h))
        return me + d + 1 < seq

    def sends_ret(d, h):
        if d == 0 and hops > 1:
            return down & jnp.logical_not(ret_via(h))
        return me - d - 1 >= 0

    def arrived_state(h):
        return pltpu.make_async_remote_copy(
            src_ref=state.at[h], dst_ref=relay_in.at[0, h],
            send_sem=state_send.at[0, h], recv_sem=relay_recv.at[0, h],
            device_id=(dp, me + 1), device_id_type=MESH,
        )

    def arrived_ret(h):
        return pltpu.make_async_remote_copy(
            src_ref=ret.at[h], dst_ref=relay_in.at[1, h],
            send_sem=ret_send.at[0, h], recv_sem=relay_recv.at[1, h],
            device_id=(dp, me - 1), device_id_type=MESH,
        )

    def relay(h):
        if hops > 1:
            @pl.when(state_relays(h))
            def _():
                arrived_state(h).wait_recv()
                relay_state(h).start()

            @pl.when(ret_relays(h))
            def _():
                arrived_ret(h).wait_recv()
                relay_ret(h).start()

    def state_sum(h):
        k32 = kf[pl.ds(h, rows, stride=heads), :]
        v16 = vf[pl.ds(h, rows, stride=heads), :].astype(jnp.bfloat16)
        kh[h] = k32.astype(jnp.bfloat16)
        vh[h] = v16
        state[h] = dot(jnp.where(in_tail, k32, 0.0).astype(jnp.bfloat16), v16, 0, 0)
        if hops > 1:
            @pl.when(state_via(h))
            def _():
                via_state(h).start()

        for d in range(hops):
            @pl.when(sends_state(d, h))
            def _(d=d):
                forward(d, h).start()

    def ret_sum(h):
        q32 = qf[pl.ds(h, rows, stride=heads), :]
        c16 = cf[pl.ds(h, rows, stride=heads), :].astype(jnp.bfloat16)
        qh[h] = q32.astype(jnp.bfloat16)
        ch[h] = c16
        ret[h] = dot(jnp.where(in_head, q32, 0.0).astype(jnp.bfloat16), c16, 0, 0)
        if hops > 1:
            @pl.when(ret_via(h))
            def _():
                via_ret(h).start()

        for d in range(hops):
            @pl.when(sends_ret(d, h))
            def _(d=d):
                backward(d, h).start()

    def each(fn):
        def body(h, _):
            fn(h)
            return 0

        return body

    ahead = min(4, heads)
    loads[0].wait()
    loads[1].wait()
    widen((k_in, kf), (v_in, vf))
    lax.fori_loop(0, ahead, each(state_sum), 0)
    loads[2].wait()
    loads[3].wait()
    widen((q_in, qf), (c_in, cf))

    def both(h):
        ret_sum(h)
        state_sum(h + ahead)

    lax.fori_loop(0, heads - ahead, each(both), 0)
    lax.fori_loop(heads - ahead, heads, each(ret_sum), 0)

    t_pos = first + lax.broadcasted_iota(jnp.int32, (rows, rows), 0)
    s_pos = first + lax.broadcasted_iota(jnp.int32, (rows, rows), 1)
    col = first + lax.broadcasted_iota(jnp.int32, (rows, 1), 0)
    begin = jnp.zeros((rows, 1), jnp.int32)
    for e in ends:
        begin = jnp.maximum(begin, jnp.where(col >= e, e, 0))
    visible = (s_pos <= t_pos) & (s_pos >= begin)
    mask[...] = jnp.where(visible, factor, 0.0).astype(jnp.float32)

    lead = heads // 8

    def inside(h, _):
        @pl.when(h >= heads // 2 - lead)
        def _():
            relay(h - (heads // 2 - lead))

        q, k, v, c = qh[h], kh[h], vh[h], ch[h]
        m = mask[...]
        weights = (m * dot(q, k, 1, 1)).astype(jnp.bfloat16)
        grad_weights = (m * dot(c, v, 1, 1)).astype(jnp.bfloat16)
        spot = pl.ds(h, rows, stride=heads)
        qf[spot, :] = dot(weights, v, 1, 0)
        kf[spot, :] = dot(grad_weights, k, 1, 0)
        vf[spot, :] = dot(grad_weights, q, 0, 0)
        cf[spot, :] = dot(weights, c, 0, 0)
        return 0

    lax.fori_loop(0, heads, inside, 0)

    head_factor = jnp.where(pos < head_end, factor, 0.0).astype(jnp.float32)
    tail_factor = jnp.where(pos >= last_start, factor, 0.0).astype(jnp.float32)

    def outside(h, _):
        carried = jnp.zeros((width, width), jnp.float32)
        returned = jnp.zeros((width, width), jnp.float32)
        @pl.when((h >= heads - heads // 2) & (h + lead < heads))
        def _():
            relay(h + lead)

        for d in range(hops):
            @pl.when(me - d - 1 >= 0)
            def _(d=d):
                forward(d, h).wait_recv()

            @pl.when(me + d + 1 < seq)
            def _(d=d):
                backward(d, h).wait_recv()

            here = head_start <= first - d * rows
            carried = carried + jnp.where(here, state_in[d, h], 0.0)
            there = last_end >= last + d * rows + 1
            returned = returned + jnp.where(there, ret_in[d, h], 0.0)
        carried = carried.astype(jnp.bfloat16)
        returned = returned.astype(jnp.bfloat16)
        q, k, v, c = qh[h], kh[h], vh[h], ch[h]
        spot = pl.ds(h, rows, stride=heads)
        qf[spot, :] = qf[spot, :] + head_factor * dot(q, carried, 1, 0)
        kf[spot, :] = kf[spot, :] + head_factor * dot(c, carried, 1, 1)
        vf[spot, :] = vf[spot, :] + tail_factor * dot(v, returned, 1, 1)
        cf[spot, :] = cf[spot, :] + tail_factor * dot(k, returned, 1, 0)
        return 0

    lax.fori_loop(0, heads, outside, 0)

    def narrow(i, _):
        at = pl.multiple_of(i * step, step)
        for src, dst in ((qf, att_out), (kf, gq_out), (vf, gk_out), (cf, gv_out)):
            block = src[pl.ds(at * heads, step * heads), :].reshape(step, heads, width)
            dst[pl.ds(at, step)] = block.astype(jnp.bfloat16)
        return 0

    lax.fori_loop(0, rows // step, narrow, 0)

    def drain(h):
        for d in range(hops):
            @pl.when(sends_state(d, h))
            def _(d=d):
                forward(d, h).wait_send()

            @pl.when(sends_ret(d, h))
            def _(d=d):
                backward(d, h).wait_send()

        if hops > 1:
            @pl.when(state_via(h))
            def _():
                via_state(h).wait_send()

            @pl.when(ret_via(h))
            def _():
                via_ret(h).wait_send()

            @pl.when(state_relays(h))
            def _():
                relay_state(h).wait_send()

            @pl.when(ret_relays(h))
            def _():
                relay_ret(h).wait_send()

    lax.fori_loop(0, heads, each(drain), 0)


def paired(
    seq,
    lens_hbm, q_hbm, k_hbm, v_hbm, c_hbm,
    o1, o2, o3, o4,
    lengths, xa_in, xb_in, pa_in, pb_in, xa_h, xb_h, pa_h, pb_h,
    mask, x_rows, p_rows, x_scale, p_scale,
    x_out, p_raw, p_sum, near_in, far_in, pair_in, relay_in, relay_sum,
    len_sem, load_sem, near_send, far_send, pair_send,
    near_recv, side_recv, pair_recv,
):
    rows, heads, width = xa_in.shape
    factor = (width * BLOCK) ** (-0.5)
    dp, me = lax.axis_index("dp"), lax.axis_index("seq")
    odd = lax.rem(me, 2) == 1
    even = jnp.logical_not(odd)
    toward = jnp.where(odd, 1, -1)
    first = me * rows
    last = first + rows - 1
    near, pair = me + toward, me - toward
    far_to, far_from = me - 2 * toward, me + 2 * toward
    near_ok = (near >= 0) & (near < seq)
    far_to_ok = (far_to >= 0) & (far_to < seq)
    far_from_ok = (far_from >= 0) & (far_from < seq)

    barrier = pltpu.get_barrier_semaphore()
    for ok, peer in ((near_ok, near), (pair >= 0, pair), (far_to_ok, far_to), (far_from_ok, far_from)):
        @pl.when(ok)
        def _(peer=peer):
            pl.semaphore_signal(barrier, inc=1, device_id=(dp, peer), device_id_type=MESH)

    parts = load_sem.shape[1]
    span = rows // parts

    len_load = pltpu.make_async_copy(lens_hbm, lengths, len_sem)
    len_load.start()

    def load(i, part, src, dst):
        cut = pl.ds(part * span, span)
        return pltpu.make_async_copy(src.at[cut], dst.at[cut], load_sem.at[i, part])

    landing = (xa_in, xb_in, pa_in, pb_in)

    @pl.when(even)
    def _():
        for pair in (0, 2):
            for part in range(parts):
                for i in (pair, pair + 1):
                    load(i, part, (q_hbm, c_hbm, k_hbm, v_hbm)[i], landing[i]).start()

    @pl.when(odd)
    def _():
        for pair in (0, 2):
            for part in range(parts):
                for i in (pair, pair + 1):
                    load(i, part, (k_hbm, v_hbm, q_hbm, c_hbm)[i], landing[i]).start()

    len_load.wait()
    big = jnp.int32(2**30)
    zero = jnp.int32(0)
    ends = []
    total = zero
    for j in range(lengths.shape[0]):
        total = total + lengths[j]
        ends.append(total)

    def start_of(p):
        out = zero
        for e in ends:
            out = jnp.maximum(out, jnp.where(e <= p, e, zero))
        return out

    def end_of(p):
        out = big
        for e in ends:
            out = jnp.minimum(out, jnp.where(e > p, e, big))
        return out

    tail_start = start_of(last + 1)
    head_end_prev = end_of(first - 1)
    head_start, head_end = start_of(first), end_of(first)
    last_start, last_end = start_of(last), end_of(last)
    x_keep = jnp.where(odd, last_end >= last + rows + 1, head_start <= first - rows)
    p_keep = jnp.where(odd, head_end_prev >= last + 1, tail_start <= first)
    relay_keep = jnp.where(odd, end_of(first - rows - 1) >= first, start_of(last + rows + 1) <= last + 1)

    pos = first + lax.broadcasted_iota(jnp.int32, (rows, width), 0)
    x_low, x_high = jnp.where(odd, tail_start, zero), jnp.where(odd, big, head_end_prev)
    p_low, p_high = jnp.where(odd, zero, tail_start), jnp.where(odd, head_end_prev, big)
    x_rows[...] = jnp.where((pos >= x_low) & (pos < x_high), 1.0, 0.0).astype(jnp.bfloat16)

    step = 16

    def widen(part, *pairs):
        def some(i, _):
            at = pl.multiple_of(part * span + i * step, step)
            for src, dst in pairs:
                block = src[pl.ds(at, step)].astype(jnp.float32)
                dst[pl.ds(at * heads, step * heads), :] = block.reshape(step * heads, width)
            return 0

        lax.fori_loop(0, span // step, some, 0)

    levels = seq // 2
    level = me // 2
    mine = jnp.where(odd, levels - 1 - level, level)
    theirs = levels - 1 - mine

    eased = (dp == 0) & even

    def my_turn(h):
        kept = (dp > 0) | even | (level > 0) | (h != heads - 2)
        return (lax.rem(h, levels) < mine) & kept

    def their_turn(h):
        kept = jnp.logical_not(eased & (level == 0) & (h == heads - 2))
        return (lax.rem(h, levels) < theirs) & kept

    def near_turn(h):
        kept = jnp.logical_not(eased & (level == 1) & (h == heads - 2))
        return (lax.rem(h, levels) < jnp.where(odd, level + 1, levels - level)) & kept

    def remote(src, dst, send, recv, peer):
        return pltpu.make_async_remote_copy(
            src_ref=src, dst_ref=dst, send_sem=send, recv_sem=recv,
            device_id=(dp, peer), device_id_type=MESH,
        )

    def direct(h):
        return remote(x_out.at[h], near_in.at[h], near_send, near_recv.at[h], near)

    def via(h):
        return remote(x_out.at[h], relay_in.at[h], near_send, side_recv.at[h], pair)

    def onward(h):
        return remote(relay_sum.at[h], near_in.at[h], far_send, near_recv.at[h], far_to)

    def far(h):
        return remote(p_raw.at[h], far_in.at[h], far_send, side_recv.at[h], far_to)

    def across(h):
        return remote(p_sum.at[h], pair_in.at[h], pair_send, pair_recv.at[h], pair)

    for part in range(parts):
        for i in (0, 1):
            load(i, part, q_hbm, landing[i]).wait()
        widen(part, (xa_in, o1), (xb_in, o2))

    pl.semaphore_wait(
        barrier, 1 + near_ok.astype(jnp.int32) + far_to_ok.astype(jnp.int32) + far_from_ok.astype(jnp.int32)
    )

    def x_state(h, _):
        spot = pl.ds(h, rows, stride=heads)
        xa = o1[spot, :].astype(jnp.bfloat16)
        xb = o2[spot, :].astype(jnp.bfloat16)
        xa_h[h] = xa
        xb_h[h] = xb

        @pl.when(near_ok)
        def _():
            x_out[h] = dot(xa * x_rows[...], xb, 0, 0)

        @pl.when(my_turn(h))
        def _():
            via(h).start()

        @pl.when(near_ok & jnp.logical_not(my_turn(h)))
        def _():
            direct(h).start()

        return 0

    lax.fori_loop(0, heads, x_state, 0)

    p_rows[...] = jnp.where((pos >= p_low) & (pos < p_high), 1.0, 0.0).astype(jnp.bfloat16)
    in_head, in_tail = pos < head_end, pos >= last_start
    head_scale = jnp.where(in_head, factor, 0.0).astype(jnp.float32)
    tail_scale = jnp.where(in_tail, factor, 0.0).astype(jnp.float32)
    x_scale[...] = jnp.where(odd, tail_scale, head_scale)
    p_scale[...] = jnp.where(odd, head_scale, tail_scale)
    col = first + lax.broadcasted_iota(jnp.int32, (1, rows), 1)
    begin = jnp.zeros((1, rows), jnp.int32)
    finish = jnp.full((1, rows), big, jnp.int32)
    for e in ends:
        begin = jnp.maximum(begin, jnp.where(col >= e, e, zero))
        finish = jnp.minimum(finish, jnp.where(col < e, e, big))
    low, high = jnp.where(odd, begin, col), jnp.where(odd, col + 1, finish)
    row = first + lax.broadcasted_iota(jnp.int32, (rows, rows), 0)
    mask[...] = jnp.where((row >= low) & (row < high), factor, 0.0).astype(jnp.float32)

    for part in range(parts):
        for i in (2, 3):
            load(i, part, q_hbm, landing[i]).wait()
        widen(part, (pa_in, o3), (pb_in, o4))

    def p_state(h):
        spot = pl.ds(h, rows, stride=heads)
        pa = o3[spot, :].astype(jnp.bfloat16)
        pb = o4[spot, :].astype(jnp.bfloat16)
        pa_h[h] = pa
        pb_h[h] = pb
        p_raw[h] = dot(pa * p_rows[...], pb, 0, 0)

        @pl.when(far_to_ok & jnp.logical_not(their_turn(h)))
        def _():
            far(h).start()

    def relay(h):
        @pl.when(their_turn(h))
        def _():
            remote(x_out.at[h], relay_in.at[h], near_send, side_recv.at[h], pair).wait_recv()
            relay_sum[h] = relay_in[h] + jnp.where(relay_keep, p_raw[h], 0.0)
            onward(h).start()

    def inner(h):
        @pl.when(near_ok)
        def _():
            direct(h).wait_recv()

        from_near = jnp.where(near_ok, near_in[h], 0.0)
        p_sum[h] = p_raw[h] + jnp.where(p_keep, from_near, 0.0)
        across(h).start()

        @pl.when(far_from_ok & jnp.logical_not(near_turn(h)))
        def _():
            far(h).wait_recv()

        use_far = x_keep & far_from_ok & jnp.logical_not(near_turn(h))
        close = (from_near + jnp.where(use_far, far_in[h], 0.0)).astype(jnp.bfloat16)
        xa, xb, pa, pb = xa_h[h], xb_h[h], pa_h[h], pb_h[h]
        m = mask[...]
        w1 = (m * dot(xa, pa, 1, 1)).astype(jnp.bfloat16)
        w2 = (m * dot(xb, pb, 1, 1)).astype(jnp.bfloat16)
        spot = pl.ds(h, rows, stride=heads)
        scale = x_scale[...]
        o1[spot, :] = dot(w1, pb, 1, 0) + scale * dot(xa, close, 1, 0)
        o2[spot, :] = dot(w2, pa, 1, 0) + scale * dot(xb, close, 1, 1)
        o3[spot, :] = dot(w2, xa, 0, 0)
        o4[spot, :] = dot(w1, xb, 0, 0)

    def outer(h):
        across(h).wait_recv()
        other = pair_in[h].astype(jnp.bfloat16)
        pa, pb = pa_h[h], pb_h[h]
        spot = pl.ds(h, rows, stride=heads)
        scale = p_scale[...]
        o3[spot, :] = o3[spot, :] + scale * dot(pb, other, 1, 1)
        o4[spot, :] = o4[spot, :] + scale * dot(pa, other, 1, 0)

    inner_lag, outer_lag = INNER_LAG + 2 * lax.rem(dp, 2), OUTER_LAG + 1

    def turn(i, _):
        @pl.when(i < heads)
        def _():
            p_state(i)
            relay(i)

        @pl.when((i >= inner_lag) & (i < heads + inner_lag))
        def _():
            inner(i - inner_lag)

        @pl.when(i >= outer_lag)
        def _():
            outer(i - outer_lag)

        return 0

    lax.fori_loop(0, heads + outer_lag, turn, 0)

    remote(p_sum, pair_in, pair_send, pair_recv.at[0], pair).wait_send()

    @pl.when(near_ok)
    def _():
        remote(x_out, near_in, near_send, near_recv.at[0], near).wait_send()

    @pl.when(far_to_ok)
    def _():
        remote(p_raw, far_in, far_send, side_recv.at[0], far_to).wait_send()


def settle(i1, i2, i3, i4, att, gq, gk, gv, s1, s2, s3, s4, sem):
    rows, heads, width = s1.shape
    parts = sem.shape[1]
    span = rows // parts
    step = 16
    odd = lax.rem(lax.axis_index("seq"), 2) == 1
    stages = (s1, s2, s3, s4)
    forward, reverse = (att, gq, gk, gv), (gv, gk, gq, att)

    def put(i, part, dst):
        cut = pl.ds(part * span, span)
        return pltpu.make_async_copy(stages[i].at[cut], dst.at[cut], sem.at[i, part])

    for part in range(parts):
        def narrow(i, _):
            at = pl.multiple_of(part * span + i * step, step)
            for src, dst in zip((i1, i2, i3, i4), stages):
                block = src[pl.ds(at * heads, step * heads), :].reshape(step, heads, width)
                dst[pl.ds(at, step)] = block.astype(jnp.bfloat16)
            return 0

        lax.fori_loop(0, span // step, narrow, 0)

        @pl.when(odd)
        def _():
            for i in range(4):
                put(i, part, reverse[i]).start()

        @pl.when(jnp.logical_not(odd))
        def _():
            for i in range(4):
                put(i, part, forward[i]).start()

    for part in range(parts):
        for i in range(4):
            put(i, part, att).wait()


def local_paired(seq, queries, keys, values, cotangent, doc_lengths):
    rows, heads, width = queries.shape
    vmem = pl.BlockSpec(memory_space=pltpu.VMEM)
    hbm = pl.BlockSpec(memory_space=pltpu.HBM)
    whole = pltpu.VMEM((rows, heads, width), jnp.bfloat16)
    by_head = pltpu.VMEM((heads, rows, width), jnp.bfloat16)
    square = pltpu.VMEM((heads, width, width), jnp.float32)
    flat = jax.ShapeDtypeStruct((rows * heads, width), jnp.float32)
    each = pltpu.SemaphoreType.DMA((heads,))
    held = pl.pallas_call(
        functools.partial(paired, seq),
        out_shape=[flat] * 4,
        in_specs=[hbm] * 5,
        out_specs=[vmem] * 4,
        scratch_shapes=[pltpu.SMEM(doc_lengths.shape, jnp.int32)]
        + [whole] * 4
        + [by_head] * 4
        + [pltpu.VMEM((rows, rows), jnp.float32)]
        + [pltpu.VMEM((rows, width), jnp.bfloat16)] * 2
        + [pltpu.VMEM((rows, width), jnp.float32)] * 2
        + [square] * 8
        + [pltpu.SemaphoreType.DMA, pltpu.SemaphoreType.DMA((4, LOAD_PARTS))]
        + [pltpu.SemaphoreType.DMA] * 3
        + [each] * 3,
        compiler_params=pltpu.CompilerParams(
            collective_id=0, has_side_effects=True, vmem_limit_bytes=40 * 2**20
        ),
    )(*(pltpu.with_memory_space_constraint(a, pltpu.HBM) for a in (doc_lengths, queries, keys, values, cotangent)))
    return pl.pallas_call(
        settle,
        out_shape=[jax.ShapeDtypeStruct(queries.shape, jnp.bfloat16)] * 4,
        in_specs=[vmem] * 4,
        out_specs=[hbm] * 4,
        scratch_shapes=[whole] * 4 + [pltpu.SemaphoreType.DMA((4, STORE_PARTS))],
        compiler_params=pltpu.CompilerParams(vmem_limit_bytes=24 * 2**20),
    )(*held)


def local(seq, queries, keys, values, cotangent, doc_lengths):
    rows, heads, width = queries.shape
    longest = seq * rows // LONGEST_PART
    hops = min(seq - 1, (longest - 1 + rows - 1) // rows)
    if hops == 2 and seq % 2 == 0:
        return local_paired(seq, queries, keys, values, cotangent, doc_lengths)
    vmem = pl.BlockSpec(memory_space=pltpu.VMEM)
    flat = pltpu.VMEM((rows * heads, width), jnp.float32)
    by_head = pltpu.VMEM((heads, rows, width), jnp.bfloat16)
    whole = pltpu.VMEM((rows, heads, width), jnp.bfloat16)
    square = pltpu.VMEM((heads, width, width), jnp.float32)
    squares = pltpu.VMEM((hops, heads, width, width), jnp.float32)
    return pl.pallas_call(
        functools.partial(kernel, seq, hops),
        out_shape=[jax.ShapeDtypeStruct(queries.shape, jnp.bfloat16)] * 4,
        in_specs=[pl.BlockSpec(memory_space=pltpu.SMEM)]
        + [pl.BlockSpec(memory_space=pltpu.HBM)] * 4,
        out_specs=[vmem] * 4,
        scratch_shapes=[whole] * 4
        + [flat] * 4
        + [by_head] * 4
        + [pltpu.VMEM((rows, rows), jnp.float32), square, square, squares, squares,
           pltpu.VMEM((2, heads, width, width), jnp.float32)]
        + [pltpu.SemaphoreType.DMA((4,)), pltpu.SemaphoreType.DMA((2, heads)), pltpu.SemaphoreType.DMA((2, heads))]
        + [pltpu.SemaphoreType.DMA((hops, heads))] * 4,
        compiler_params=pltpu.CompilerParams(
            collective_id=0, has_side_effects=True, vmem_limit_bytes=49 * 2**20
        ),
    )(doc_lengths, queries, keys, values, cotangent)


def solution(mesh):
    spec = P(("dp", "seq"), None, None)
    return jax.shard_map(
        functools.partial(local, mesh.shape["seq"]),
        mesh=mesh,
        in_specs=(spec, spec, spec, spec, P("dp")),
        out_specs=(spec, spec, spec, spec),
        check_vma=False,
    )
```
